32 devices in a mesh: parts: 2 (over y), seq: 4 (over z), tok: 2 (over x), head: 2 (over core).
Axes of the slice: x: 2, y: 2, z: 4, core: 2. Of those that a mesh axis runs over, the one named last changes fastest.
Arguments:
- values: bfloat16 [8192, 2048], P(('parts', 'seq', 'tok'), 'head'), parts along dimension 0, may hold values from -6 to 6
- key_rows: bfloat16 [8192, 128], P(('parts', 'seq', 'tok')), parts along dimension 0, may hold values from -0.5 to 0.5
- query_rows: bfloat16 [8192, 128], P(('parts', 'seq', 'tok')), parts along dimension 0, may hold values from -6 to 6
- decay_codes: int32 [32, 8192], P('head', ('parts', 'seq', 'tok')), parts along dimension 1, may hold values from 0 to 48398, as said below
- weight_codes: int32 [12, 32, 8192], P(None, 'head', ('parts', 'seq', 'tok')), parts along dimension 2, may hold values from 16 to 511
- norm_gain: float32 [2048], P('head'), may hold values from 0.5 to 1.5
Outputs:
- mixed: bfloat16 [8192, 2048], P(('parts', 'seq', 'tok'), 'head'), parts along dimension 0
The draws below stay inside these ranges and needn't reach their ends.
There are 2 independent parts, one for each index of `parts`. The reference program is written for one: setup_inputs(seed, part) draws one part's arguments, and reference() takes and returns one part's arrays. A program takes and returns all parts, laid end to end along the dimension named above; an argument that names none is the same for every part. Nothing has to cross between parts.
Inputs may be any that keep to these rules, and one draw needn't show every extreme that they name: `decay_codes`: Log-decay numerators over 65536. `weight_codes`: level weight numerators over 256.
All inputs are finite; a program needn't handle non-finite values.
Results may differ from the reference program's by a relative error of at most 0.0048.
Values sent between devices are 32-bit elements; how exact they have to be, the bound alone decides.
A program may use at most 64 MiB of HBM per device.

```python
import jax
import jax.numpy as jnp
from jax import lax

HEAD_TOTAL = 32
P_SIZE = 64
N = 128
BUCKET = 64
LEVELS = 12
TOK_DEV = 512
TOKEN_TOTAL = 4096
N_SEQ = 4
N_TOK = 2


def draw_decay_codes(key, part):
    random_seed_key = jax.random.fold_in(key, 7)
    selector_random_key, gradual_random_key, quick_random_key, position_random_key, spike_random_key = jax.random.split(random_seed_key, 5)
    quick_head_flags = jax.random.randint(selector_random_key, (HEAD_TOTAL, 1), 0, 2)
    gradual_decay_labels = jax.random.randint(gradual_random_key, (HEAD_TOTAL, TOKEN_TOTAL), 0, 1 + 131072 // TOKEN_TOTAL)
    quick_decay_labels = jax.random.randint(quick_random_key, (HEAD_TOTAL, TOKEN_TOTAL), 1000, 3000)
    spike_positions = jax.random.randint(position_random_key, (4,), 0, TOKEN_TOTAL)
    spike_position = jnp.any(jnp.arange(TOKEN_TOTAL)[:, None] == spike_positions[None, :], axis=1)
    spike_decay_labels = jax.random.randint(spike_random_key, (HEAD_TOTAL, TOKEN_TOTAL), 14600, 45400)
    return jnp.where(quick_head_flags == 1, quick_decay_labels, gradual_decay_labels) + jnp.where(spike_position[None, :], spike_decay_labels, 0)


def plant(entries, own_key, least, largest):
    spot = [jax.random.randint(jax.random.fold_in(own_key, axis), (), 0, length) for axis, length in enumerate(entries.shape)]
    main_axis = entries.shape.index(max(entries.shape))
    beside = spot[:main_axis] + [(spot[main_axis] + 1) % entries.shape[main_axis]] + spot[main_axis + 1:]
    return entries.at[tuple(spot)].set(least).at[tuple(beside)].set(largest)


def shard_levels(own_key, extent, cuts, low, top_value):
    gain = 1.0
    for position, parts in cuts:
        heights = jax.random.uniform(jax.random.fold_in(jax.random.fold_in(own_key, 6), position), (parts,), jnp.float32, low / len(cuts), top_value / len(cuts))
        gain = gain * jnp.repeat(jnp.exp(heights), extent[position] // parts).reshape((-1,) + (1,) * (len(extent) - 1 - position))
    return gain


def noise(rng, dims, scale, bound, cuts=(), held_as=jnp.bfloat16):
    values = scale * jax.random.normal(rng, dims, jnp.float32)
    if cuts:
        values = values * shard_levels(rng, dims, cuts, -0.22, 0.18)
    return jnp.clip(values, -bound, bound).astype(held_as)


def setup_inputs(seed: int = 0, part: int = 0) -> dict:
    streams_of = jax.random.split(jax.random.key(seed), 7)
    part_keys = jax.random.split(jax.random.fold_in(streams_of[6], part), 7)
    return {
        "values": noise(part_keys[0], (TOKEN_TOTAL, HEAD_TOTAL * P_SIZE), 1.0, 6.0, ((0, 8), (1, 2))),
        "key_rows": noise(part_keys[1], (TOKEN_TOTAL, N), N ** -0.5, 0.5, ((0, 8),)),
        "query_rows": noise(part_keys[2], (TOKEN_TOTAL, N), 1.0, 6.0, ((0, 8),)),
        "decay_codes": draw_decay_codes(jax.random.fold_in(jax.random.fold_in(streams_of[6], part), 71), part),
        "weight_codes": plant(jax.random.randint(part_keys[4], (LEVELS, HEAD_TOTAL, TOKEN_TOTAL), 16, 512), jax.random.fold_in(part_keys[4], 1), 16, 511).astype(jnp.int32),
        "norm_gain": jnp.clip(1.0 + 0.1 * jax.random.normal(streams_of[5], (HEAD_TOTAL * P_SIZE,), jnp.float32), 0.5, 1.5),
    }


decay_denominator = 65536.0
weight_denominator = 256.0
norm_epsilon = 1e-05
row_limit = 512
highest = lax.Precision.HIGHEST

def bit_count(numbers, width_bits):
    result = jnp.zeros(numbers.shape, jnp.int32)
    for bit_place in range(width_bits):
        result = result + (numbers >= 1 << bit_place).astype(jnp.int32)
    return result

def token_spread(levels_full, lam_rows, slot_count):
    spread = jnp.zeros(levels_full.shape, jnp.float32)
    for slot in range(slot_count):
        spread = spread + jnp.where(levels_full == slot, lam_rows[slot][:, None], 0.0)
    return spread

def decay_sums(decay_codes):
    return jnp.cumsum(-decay_codes.astype(jnp.float32) / decay_denominator, axis=1)

def near_terms(values, key_rows, query_rows, cumulative, level_scale, head_size):
    token_count = values.shape[0]
    head_count = cumulative.shape[0]
    buckets = token_count // BUCKET
    level_bits = (buckets - 1).bit_length()
    bucket_ids = jnp.arange(buckets, dtype=jnp.int32)
    levels = bit_count(jnp.bitwise_xor(bucket_ids[:, None], bucket_ids[None, :]), level_bits)
    head_weights = jnp.transpose(level_scale[:level_bits + 1], (1, 0, 2))
    block_rows = min(row_limit, token_count)
    pieces = []
    for row_start in range(0, token_count, block_rows):
        row_end = row_start + block_rows
        scores = jnp.einsum('tn,sn->ts', query_rows[row_start:row_end], key_rows[:row_end], preferred_element_type=jnp.float32)
        causal = jnp.arange(row_start, row_end)[:, None] >= jnp.arange(row_end)[None, :]
        tiles = levels[row_start // BUCKET:row_end // BUCKET, :row_end // BUCKET]
        levels_full = jnp.broadcast_to(tiles[:, None, :, None], (block_rows // BUCKET, BUCKET, row_end // BUCKET, BUCKET)).reshape(block_rows, row_end)

        def one_head(head_item):
            cum_rates, weights, head_index = head_item
            log_gap = jnp.where(causal, cum_rates[row_start:row_end, None] - cum_rates[None, :row_end], 0.0)
            spread = token_spread(levels_full, weights[:, row_start:row_end], level_bits + 1)
            mixing = jnp.where(causal, jnp.exp(log_gap) * spread * scores, 0.0).astype(jnp.bfloat16)
            columns = lax.dynamic_slice_in_dim(values[:row_end], head_index * head_size, head_size, 1)
            return jnp.dot(mixing, columns, preferred_element_type=jnp.float32)
        pieces.append(lax.map(one_head, (cumulative, head_weights, jnp.arange(head_count, dtype=jnp.int32))))
    return jnp.concatenate(pieces, axis=1)

def block_state(values, key_rows, cumulative, head_size):
    token_count = values.shape[0]
    head_count = cumulative.shape[0]
    end_decay = jnp.exp(cumulative[:, -1:] - cumulative)
    decayed = (values.astype(jnp.float32).reshape(token_count, head_count, head_size) * end_decay.T[:, :, None]).astype(jnp.bfloat16)
    return jnp.einsum('tn,thp->hnp', key_rows, decayed, preferred_element_type=jnp.float32)

def decay_coeff(sources, own_index, log_gap):
    earlier = (sources < own_index)[:, None]
    return jnp.where(earlier, jnp.exp(jnp.where(earlier, log_gap, 0.0)), 0.0)

def level_onehot(levels, slot_ids):
    return (levels[:, None] == slot_ids[None, :]).astype(jnp.float32)

def finish(near, far_levels, far_weights, query_rows, cumulative, norm_gain, head_size):
    token_count = query_rows.shape[0]
    head_count = cumulative.shape[0]
    queries = query_rows.astype(jnp.float32)
    readout = jnp.zeros(near.shape, jnp.float32)
    for slot in range(far_levels.shape[0]):
        part_out = jnp.einsum('tn,hnp->htp', queries, far_levels[slot], precision=highest)
        readout = readout + far_weights[slot][:, :, None] * part_out
    combined = near + jnp.exp(cumulative)[:, :, None] * readout
    inverse_rms = lax.rsqrt(lax.optimization_barrier(jnp.mean(combined * combined, axis=2, keepdims=True)) + norm_epsilon)
    normed = combined * inverse_rms * norm_gain.astype(jnp.float32).reshape(head_count, 1, head_size)
    return jnp.transpose(normed, (1, 0, 2)).reshape(token_count, head_count * head_size).astype(jnp.bfloat16)

def reference(values, key_rows, query_rows, decay_codes, weight_codes, norm_gain):
    devices = N_SEQ * N_TOK
    value_blocks = values.reshape(devices, TOK_DEV, HEAD_TOTAL * P_SIZE)
    key_blocks = key_rows.reshape(devices, TOK_DEV, N)
    query_blocks = query_rows.reshape(devices, TOK_DEV, N)
    code_blocks = jnp.transpose(decay_codes.reshape(HEAD_TOTAL, devices, TOK_DEV), (1, 0, 2))
    weight_blocks = jnp.transpose(weight_codes.reshape(LEVELS, HEAD_TOTAL, devices, TOK_DEV), (2, 0, 1, 3))

    def state_of(block_item):
        block_values, block_keys, block_codes = block_item
        cumulative = decay_sums(block_codes)
        return (block_state(block_values, block_keys, cumulative, P_SIZE), cumulative[:, -1])
    states, totals = lax.map(state_of, (value_blocks, key_blocks, code_blocks))
    inclusive = jnp.cumsum(totals, axis=0)
    exclusive = inclusive - totals
    base_level = (TOK_DEV // BUCKET).bit_length() - 1
    device_bits = (devices - 1).bit_length()
    sources = jnp.arange(devices, dtype=jnp.int32)
    slot_ids = base_level + 1 + jnp.arange(device_bits, dtype=jnp.int32)

    def output_of(block_item):
        block_index, block_values, block_keys, block_queries, block_codes, block_weights = block_item
        cumulative = decay_sums(block_codes)
        level_scale = block_weights.astype(jnp.float32) / weight_denominator
        near = near_terms(block_values, block_keys, block_queries, cumulative, level_scale, P_SIZE)
        log_gap = exclusive[block_index][None, :] - inclusive
        coefficient = decay_coeff(sources, block_index, log_gap)
        levels = base_level + bit_count(jnp.bitwise_xor(sources, block_index), device_bits)
        onehot = level_onehot(levels, slot_ids)
        far_levels = jnp.einsum('mh,mj,mhnp->jhnp', coefficient, onehot, states, precision=highest)
        far_weights = level_scale[base_level + 1:base_level + 1 + device_bits]
        return finish(near, far_levels, far_weights, block_queries, cumulative, norm_gain, P_SIZE)
    outputs = lax.map(output_of, (sources, value_blocks, key_blocks, query_blocks, code_blocks, weight_blocks))
    return outputs.reshape(TOKEN_TOTAL, HEAD_TOTAL * P_SIZE)
```

```python
import functools

import jax
import jax.numpy as jnp
from jax import lax
from jax.experimental import pallas as pl
from jax.experimental.pallas import tpu as pltpu
from jax.sharding import PartitionSpec as P

BUCKET = 64
F32 = jnp.float32
BF16 = jnp.bfloat16
MESH = pl.DeviceIdType.MESH
EXTRA = 8


def mm(a, b):
    return jnp.dot(a, b, preferred_element_type=F32)


def tmm(a, b):
    return lax.dot_general(a, b, (((0,), (0,)), ((), ())), preferred_element_type=F32)


def kernel(
    dims, v_ref, k_ref, q_ref, codes_ref, w_ref, g_ref, o_ref,
    acc, items, sel, scores, own_scores, q_twice, pref, agg, from_tok, from_seq, chain,
    tok_send, tok_recv, seq_send, seq_recv,
):
    tok_bits, seq_bits, head_size, chunk = dims
    heads, tokens = codes_ref.shape
    columns = v_ref.shape[1]
    states = k_ref.shape[1]
    chunks = columns // chunk
    near_levels = (tokens // BUCKET).bit_length() - 1
    per_group = 128 // (2 * heads)
    tok = lax.axis_index("tok")
    seq = lax.axis_index("seq")
    seq_count = 2**seq_bits
    has_next = seq + 1 < seq_count
    has_prev = seq > 0

    barrier = pltpu.get_barrier_semaphore()
    for bit in range(tok_bits):
        pl.semaphore_signal(
            barrier, inc=1, device_id={"tok": tok ^ (1 << bit)}, device_id_type=MESH
        )

    @pl.when(has_next)
    def _():
        pl.semaphore_signal(barrier, inc=1, device_id={"seq": seq + 1}, device_id_type=MESH)

    @pl.when(has_prev)
    def _():
        pl.semaphore_signal(barrier, inc=1, device_id={"seq": seq - 1}, device_id_type=MESH)

    def tok_copy(bit, c):
        return pltpu.make_async_remote_copy(
            src_ref=agg.at[bit, c],
            dst_ref=from_tok.at[bit, c],
            send_sem=tok_send.at[bit, c],
            recv_sem=tok_recv.at[bit, c],
            device_id={"tok": tok ^ (1 << bit)},
            device_id_type=MESH,
        )

    def seq_copy(source, slot, c):
        return pltpu.make_async_remote_copy(
            src_ref=source,
            dst_ref=from_seq.at[slot, c],
            send_sem=seq_send.at[slot, c],
            recv_sem=seq_recv.at[slot, c],
            device_id={"seq": lax.rem(seq + 1, seq_count)},
            device_id_type=MESH,
        )

    def cols(c):
        return slice(c * chunk, (c + 1) * chunk)

    lane = lax.broadcasted_iota(jnp.int32, (heads, tokens), 1)
    run_total = codes_ref[...]
    prefix = run_total
    before, after = {}, {}
    size = 1
    while True:
        if size >= BUCKET:
            before[size] = prefix.astype(F32) * (-1.0 / 65536.0)
            after[size] = (run_total - prefix).astype(F32) * (-1.0 / 65536.0)
        if size == tokens:
            break
        upper = (lane & size) != 0
        lower_total = pltpu.roll(run_total, size, 1)
        upper_total = pltpu.roll(run_total, tokens - size, 1)
        prefix = prefix + jnp.where(upper, lower_total, 0)
        run_total = run_total + jnp.where(upper, lower_total, upper_total)
        size *= 2
    block_total = run_total.astype(F32) * (-1.0 / 65536.0)

    row = lax.broadcasted_iota(jnp.int32, (128, columns), 0)
    column_head = lax.broadcasted_iota(jnp.int32, (128, columns), 1) // head_size
    for i in range(per_group):
        wanted = (row // (2 * heads) == i) & (row % heads == column_head)
        sel[i] = jnp.where(wanted, 1.0, 0.0).astype(BF16)
    total_row = jnp.sum(
        jnp.where(
            lax.broadcasted_iota(jnp.int32, (heads, columns), 0)
            == lax.broadcasted_iota(jnp.int32, (heads, columns), 1) // head_size,
            block_total[:, :1],
            0.0,
        ),
        axis=0,
        keepdims=True,
    )

    def put_items(group, entries):
        halves = []
        for entry in entries:
            high = entry.astype(BF16).astype(F32)
            halves += [high, entry - high]
        short = per_group - len(entries)
        if short:
            halves.append(jnp.zeros((2 * heads * short, tokens), F32))
        items[group] = jnp.transpose(jnp.concatenate(halves, axis=0)).astype(BF16)

    def spread(index, c, start=0, stop=None):
        group, i = index // per_group, index % per_group
        stop = tokens if stop is None else stop
        return mm(items[group, start:stop, :], sel[i, :, cols(c)])

    sizes = [tokens] + [BUCKET << i for i in range(near_levels)]
    key_entries = [jnp.exp(after[s]) for s in sizes]
    key_groups = -(-len(key_entries) // per_group)
    for g in range(key_groups):
        put_items(g, key_entries[g * per_group : (g + 1) * per_group])
    key_item = {s: i for i, s in enumerate(sizes)}

    pl.semaphore_wait(
        barrier, tok_bits + has_next.astype(jnp.int32) + has_prev.astype(jnp.int32)
    )
    for c in range(chunks):
        decayed = (v_ref[:, cols(c)].astype(F32) * spread(0, c)).astype(BF16)
        agg[0, c, :states, :] = tmm(k_ref[...], decayed)
        agg[0, c, states:, :] = jnp.broadcast_to(total_row[:, cols(c)], (EXTRA, chunk))
        if tok_bits:
            tok_copy(0, c).start()

    def lam(level):
        return w_ref[level].astype(F32) * (1.0 / 256.0)

    read_entries = [lam(0) * jnp.exp(-after[BUCKET])]
    for level in range(1, near_levels + 1):
        read_entries.append(lam(level) * jnp.exp(before[BUCKET << (level - 1)]))
    since_start = jnp.exp(before[tokens])
    for level in range(near_levels + 1, near_levels + 1 + tok_bits + seq_bits):
        read_entries.append(lam(level) * since_start)
    read_base = key_groups * per_group
    for g in range(-(-len(read_entries) // per_group)):
        put_items(key_groups + g, read_entries[g * per_group : (g + 1) * per_group])

    products = lax.dot_general(
        q_ref[...], k_ref[...], (((1,), (1,)), ((), ())), preferred_element_type=F32
    )
    scores[...] = products.astype(BF16)
    t_id = lax.broadcasted_iota(jnp.int32, (tokens, tokens), 0)
    s_id = lax.broadcasted_iota(jnp.int32, (tokens, tokens), 1)
    in_bucket = (t_id // BUCKET == s_id // BUCKET) & (t_id >= s_id)
    own_scores[...] = jnp.where(in_bucket, products, 0.0).astype(BF16)
    q_twice[:, :states] = q_ref[...]
    q_twice[:, states:] = q_ref[...]

    def near(c):
        here = v_ref[:, cols(c)].astype(F32)
        by_bucket = (here * spread(key_item[BUCKET], c)).astype(BF16)
        block = min(256, tokens)
        for start in range(0, tokens, block):
            rows = slice(start, start + block)
            acc[rows, cols(c)] = mm(own_scores[rows, rows], by_bucket[rows]) * spread(
                read_base, c, start, start + block
            )
        for level in range(1, near_levels + 1):
            half = BUCKET << (level - 1)
            for start in range(0, tokens, 2 * half):
                low = slice(start, start + half)
                high = slice(start + half, start + 2 * half)
                if half == BUCKET:
                    source = by_bucket[low]
                else:
                    source = (
                        here[low] * spread(key_item[half], c, start, start + half)
                    ).astype(BF16)
                acc[high, cols(c)] += mm(scores[high, low], source) * spread(
                    read_base + level, c, start + half, start + 2 * half
                )

    def far(level, payload, gap, c):
        state = payload[:states] * jnp.exp(gap)
        high = state.astype(BF16)
        low = (state - high.astype(F32)).astype(BF16)
        acc[:, cols(c)] += mm(q_twice[...], jnp.concatenate([high, low], axis=0)) * spread(
            read_base + level, c
        )

    trailing = [
        (seq & ((1 << (t + 1)) - 1)) == (1 << t) - 1 for t in range(seq_bits)
    ]

    def tok_step(bit, c):
        tok_copy(bit, c).wait_recv()
        upper = ((tok >> bit) & 1) == 1
        mine, theirs = agg.at[bit, c], from_tok.at[bit, c]
        my_total, their_total = mine[states:][:1], theirs[states:][:1]

        @pl.when(upper)
        def _():
            agg[bit + 1, c, :states] = jnp.exp(my_total) * theirs[:states] + mine[:states]

        @pl.when(jnp.logical_not(upper))
        def _():
            agg[bit + 1, c, :states] = jnp.exp(their_total) * mine[:states] + theirs[:states]

        agg[bit + 1, c, states:] = jnp.broadcast_to(my_total + their_total, (EXTRA, chunk))
        if bit + 1 < tok_bits:
            tok_copy(bit + 1, c).start()

    def tok_read(bit, c):
        @pl.when(((tok >> bit) & 1) == 1)
        def _():
            far(near_levels + 1 + bit, from_tok.at[bit, c], pref[c, :1], c)
            pref[c] += from_tok[bit, c, states:]

    for c in range(chunks):
        pref[c] = jnp.zeros((EXTRA, chunk), F32)
    for bit in range(max(tok_bits, 1)):
        for c in range(chunks):
            if bit == 0:
                near(c)
            if bit < tok_bits:
                tok_step(bit, c)
            if bit + 1 >= tok_bits and seq_bits:

                @pl.when(jnp.logical_and(has_next, trailing[0]))
                def _():
                    seq_copy(agg.at[tok_bits, c], 0, c).start()

    for bit in range(tok_bits):
        for c in range(chunks):
            tok_read(bit, c)

    def seq_step(slot, c):
        @pl.when(((seq >> slot) & 1) == 1)
        def _():
            seq_copy(agg.at[tok_bits, c], slot, c).wait_recv()

            @pl.when(jnp.logical_and(has_next, ((seq + 1) >> slot) == (seq >> slot)))
            def _():
                seq_copy(from_seq.at[slot, c], slot, c).start()

            if slot + 1 < seq_bits:

                @pl.when(jnp.logical_and(has_next, trailing[slot + 1]))
                def _():
                    total = agg[tok_bits, c, states:][:1]
                    state = agg[tok_bits, c, :states]
                    for lower in range(slot + 1):
                        state = state + jnp.exp(total) * from_seq[lower, c, :states]
                        total = total + from_seq[lower, c, states:][:1]
                    chain[c, :states] = state
                    chain[c, states:] = jnp.broadcast_to(total, (EXTRA, chunk))
                    seq_copy(chain.at[c], slot + 1, c).start()

            far(near_levels + 1 + tok_bits + slot, from_seq.at[slot, c], pref[c, :1], c)
            pref[c] += from_seq[slot, c, states:]

    group_row = lax.broadcasted_iota(jnp.int32, (chunk, chunk), 0) // head_size
    group_col = lax.broadcasted_iota(jnp.int32, (chunk, chunk), 1) // head_size
    same_head = jnp.where(group_row == group_col, 1.0, 0.0).astype(BF16)

    def norm(c):
        y = acc[:, cols(c)]
        mean = mm((y * y).astype(BF16), same_head) * (1.0 / head_size)
        o_ref[:, cols(c)] = (y * lax.rsqrt(mean + 1e-5) * g_ref[:, cols(c)]).astype(o_ref.dtype)

    for slot in range(seq_bits):
        for c in range(chunks):
            seq_step(slot, c)
            if slot == seq_bits - 1:
                norm(c)
    if not seq_bits:
        for c in range(chunks):
            norm(c)

    for bit in range(tok_bits):
        for c in range(chunks):
            tok_copy(bit, c).wait_send()
    for slot in range(seq_bits):
        for c in range(chunks):

            @pl.when(jnp.logical_and(has_next, (((seq + 1) >> slot) & 1) == 1))
            def _():
                seq_copy(from_seq.at[slot, c], slot, c).wait_send()


def local(values, key_rows, query_rows, decay_codes, weight_codes, norm_gain):
    heads, tokens = decay_codes.shape
    columns = values.shape[1]
    states = key_rows.shape[1]
    head_size = columns // heads
    chunk = min(256, columns)
    chunks = columns // chunk
    tok_bits = lax.axis_size("tok").bit_length() - 1
    seq_bits = lax.axis_size("seq").bit_length() - 1
    near_levels = (tokens // BUCKET).bit_length() - 1
    per_group = 128 // (2 * heads)
    groups = -(-(near_levels + 1) // per_group) - (
        -(near_levels + 1 + tok_bits + seq_bits) // per_group
    )
    parcel = (chunks, states + EXTRA, chunk)
    vmem = pl.BlockSpec(memory_space=pltpu.VMEM)
    return pl.pallas_call(
        functools.partial(kernel, (tok_bits, seq_bits, head_size, chunk)),
        out_shape=jax.ShapeDtypeStruct((tokens, columns), values.dtype),
        in_specs=[vmem] * 6,
        out_specs=vmem,
        scratch_shapes=[
            pltpu.VMEM((tokens, columns), F32),
            pltpu.VMEM((groups, tokens, 128), BF16),
            pltpu.VMEM((per_group, 128, columns), BF16),
            pltpu.VMEM((tokens, tokens), BF16),
            pltpu.VMEM((tokens, tokens), BF16),
            pltpu.VMEM((tokens, 2 * states), BF16),
            pltpu.VMEM((chunks, EXTRA, chunk), F32),
            pltpu.VMEM((tok_bits + 1,) + parcel, F32),
            pltpu.VMEM((max(tok_bits, 1),) + parcel, F32),
            pltpu.VMEM((max(seq_bits, 1),) + parcel, F32),
            pltpu.VMEM(parcel, F32),
            pltpu.SemaphoreType.DMA((max(tok_bits, 1), chunks)),
            pltpu.SemaphoreType.DMA((max(tok_bits, 1), chunks)),
            pltpu.SemaphoreType.DMA((max(seq_bits, 1), chunks)),
            pltpu.SemaphoreType.DMA((max(seq_bits, 1), chunks)),
        ],
        compiler_params=pltpu.CompilerParams(collective_id=0, has_side_effects=True),
    )(values, key_rows, query_rows, decay_codes, weight_codes, norm_gain.reshape(1, columns))


def solution(mesh):
    return jax.shard_map(
        local,
        mesh=mesh,
        in_specs=(
            P(("parts", "seq", "tok"), "head"),
            P(("parts", "seq", "tok"), None),
            P(("parts", "seq", "tok"), None),
            P("head", ("parts", "seq", "tok")),
            P(None, "head", ("parts", "seq", "tok")),
            P("head"),
        ),
        out_specs=P(("parts", "seq", "tok"), "head"),
        check_vma=False,
    )
```

```python
import functools

import jax
import jax.numpy as jnp
from jax import lax
from jax.experimental import pallas as pl
from jax.experimental.pallas import tpu as pltpu
from jax.sharding import PartitionSpec as P

BUCKET = 64
F32 = jnp.float32
BF16 = jnp.bfloat16
MESH = pl.DeviceIdType.MESH
LANES = 128


def mm(a, b):
    return jnp.dot(a, b, preferred_element_type=F32)


def tmm(a, b):
    return lax.dot_general(a, b, (((0,), (0,)), ((), ())), preferred_element_type=F32)


def kernel(
    dims, v_hbm, k_hbm, q_hbm, codes_hbm, w_hbm, o_ref,
    v_ref, k_ref, q_ref, codes_ref, w_ref, load_sem,
    acc, items, sel, scores, own_scores, q_twice, agg, from_tok, from_seq, chain,
    pref, agg_total, tok_total, seq_total, chain_total,
    tok_send, tok_recv, seq_send, seq_recv, swap_send, swap_recv,
):
    tok_bits, seq_bits, head_size, chunk = dims
    heads, tokens = codes_ref.shape
    columns = v_ref.shape[1]
    states = k_ref.shape[1]
    chunks = columns // chunk
    near_levels = (tokens // BUCKET).bit_length() - 1
    per_group = 128 // (2 * heads)
    tok = lax.axis_index("tok")
    seq = lax.axis_index("seq")
    seq_count = 2**seq_bits
    has_next = seq + 1 < seq_count
    has_prev = seq > 0

    def load(i):
        source, target = (
            (codes_hbm, codes_ref), (k_hbm, k_ref), (v_hbm, v_ref), (q_hbm, q_ref), (w_hbm, w_ref)
        )[i]
        return pltpu.make_async_copy(source, target, load_sem.at[i])

    for i in range(5):
        load(i).start()

    barrier = pltpu.get_barrier_semaphore()
    for bit in range(tok_bits):
        pl.semaphore_signal(
            barrier, inc=1, device_id={"tok": tok ^ (1 << bit)}, device_id_type=MESH
        )

    @pl.when(has_next)
    def _():
        pl.semaphore_signal(barrier, inc=1, device_id={"seq": seq + 1}, device_id_type=MESH)

    @pl.when(has_prev)
    def _():
        pl.semaphore_signal(barrier, inc=1, device_id={"seq": seq - 1}, device_id_type=MESH)

    half = states // 2
    mine_at = pl.multiple_of((tok & 1) * half, half)
    other_at = pl.multiple_of((1 - (tok & 1)) * half, half)
    after_me = lax.rem(seq + 1, seq_count)

    def splits(slot):
        return slot > 0 and tok_bits > 0

    def tok_copy(bit, c):
        totals = c == chunks
        return pltpu.make_async_remote_copy(
            src_ref=agg_total.at[bit] if totals else agg.at[bit, c],
            dst_ref=tok_total.at[bit] if totals else from_tok.at[bit, c],
            send_sem=tok_send.at[bit, c],
            recv_sem=tok_recv.at[bit, c],
            device_id={"tok": tok ^ (1 << bit)},
            device_id_type=MESH,
        )

    def seq_copy(source, slot, c):
        if c == chunks:
            target = seq_total.at[slot]
        else:
            target = from_seq.at[slot, c]
            if splits(slot):
                source = source.at[pl.ds(mine_at, half)]
                target = target.at[pl.ds(mine_at, half)]
        return pltpu.make_async_remote_copy(
            src_ref=source,
            dst_ref=target,
            send_sem=seq_send.at[slot, c],
            recv_sem=seq_recv.at[slot, c],
            device_id={"seq": after_me},
            device_id_type=MESH,
        )

    def swap_copy(slot, c, at):
        place = from_seq.at[slot, c, pl.ds(at, half)]
        return pltpu.make_async_remote_copy(
            src_ref=place,
            dst_ref=place,
            send_sem=swap_send.at[slot, c],
            recv_sem=swap_recv.at[slot, c],
            device_id={"tok": tok ^ 1},
            device_id_type=MESH,
        )

    pieces = chunk // LANES

    def row_of(total, c):
        return jnp.concatenate(
            [total[c * pieces + i : c * pieces + i + 1, :] for i in range(pieces)], axis=1
        )

    def cols(c):
        return slice(c * chunk, (c + 1) * chunk)

    load(0).wait()
    lane = lax.broadcasted_iota(jnp.int32, (heads, tokens), 1)
    run_total = codes_ref[...]
    prefix = run_total
    before, after = {}, {}
    size = 1
    while True:
        if size >= BUCKET:
            before[size] = prefix.astype(F32) * (-1.0 / 65536.0)
            after[size] = (run_total - prefix).astype(F32) * (-1.0 / 65536.0)
        if size == tokens:
            break
        upper = (lane & size) != 0
        lower_total = pltpu.roll(run_total, size, 1)
        upper_total = pltpu.roll(run_total, tokens - size, 1)
        prefix = prefix + jnp.where(upper, lower_total, 0)
        run_total = run_total + jnp.where(upper, lower_total, upper_total)
        size *= 2
    block_total = run_total.astype(F32) * (-1.0 / 65536.0)

    head_shift = head_size.bit_length() - 1
    item_shift = (2 * heads).bit_length() - 1

    def put_sel(i):
        row = lax.broadcasted_iota(jnp.int32, (LANES, columns), 0)
        column_head = lax.broadcasted_iota(jnp.int32, (LANES, columns), 1) >> head_shift
        wanted = ((row >> item_shift) == i) & ((row & (heads - 1)) == column_head)
        sel[i] = jnp.where(wanted, 1.0, 0.0).astype(BF16)

    put_sel(0)
    total_row = jnp.sum(
        jnp.where(
            lax.broadcasted_iota(jnp.int32, (heads, columns), 0)
            == lax.broadcasted_iota(jnp.int32, (heads, columns), 1) >> head_shift,
            block_total[:, :1],
            0.0,
        ),
        axis=0,
        keepdims=True,
    )

    def put_items(group, entries):
        halves = []
        for entry in entries:
            high = entry.astype(BF16).astype(F32)
            halves += [high, entry - high]
        short = per_group - len(entries)
        if short:
            halves.append(jnp.zeros((2 * heads * short, tokens), F32))
        items[group] = jnp.transpose(jnp.concatenate(halves, axis=0)).astype(BF16)

    def spread(index, c, start=0, stop=None):
        group, i = index // per_group, index % per_group
        stop = tokens if stop is None else stop
        return mm(items[group, start:stop, :], sel[i, :, cols(c)])

    sizes = [tokens] + [BUCKET << i for i in range(near_levels)]
    key_entries = [jnp.exp(after[s]) for s in sizes]
    key_groups = -(-len(key_entries) // per_group)
    for g in range(key_groups):
        put_items(g, key_entries[g * per_group : (g + 1) * per_group])
    key_item = {s: i for i, s in enumerate(sizes)}

    for r in range(columns // LANES):
        agg_total[0, r : r + 1] = total_row[:, r * LANES : (r + 1) * LANES]
    load(1).wait()
    load(2).wait()
    pl.semaphore_wait(
        barrier, tok_bits + has_next.astype(jnp.int32) + has_prev.astype(jnp.int32)
    )
    for c in range(chunks):
        decayed = (v_ref[:, cols(c)].astype(F32) * spread(0, c)).astype(BF16)
        agg[0, c] = tmm(k_ref[...], decayed)
        if tok_bits:
            if c == 0:
                tok_copy(0, chunks).start()
            tok_copy(0, c).start()
    for i in range(1, per_group):
        put_sel(i)

    load(3).wait()
    load(4).wait()

    def lam(level):
        return w_ref[level].astype(F32) * (1.0 / 256.0)

    read_entries = [lam(0) * jnp.exp(-after[BUCKET])]
    for level in range(1, near_levels + 1):
        read_entries.append(lam(level) * jnp.exp(before[BUCKET << (level - 1)]))
    since_start = jnp.exp(before[tokens])
    for level in range(near_levels + 1, near_levels + 1 + tok_bits + seq_bits):
        read_entries.append(lam(level) * since_start)
    read_base = key_groups * per_group
    for g in range(-(-len(read_entries) // per_group)):
        put_items(key_groups + g, read_entries[g * per_group : (g + 1) * per_group])

    products = lax.dot_general(
        q_ref[...], k_ref[...], (((1,), (1,)), ((), ())), preferred_element_type=F32
    )
    scores[...] = products.astype(BF16)
    t_id = lax.broadcasted_iota(jnp.int32, (tokens, tokens), 0)
    s_id = lax.broadcasted_iota(jnp.int32, (tokens, tokens), 1)
    bucket_shift = BUCKET.bit_length() - 1
    in_bucket = ((t_id >> bucket_shift) == (s_id >> bucket_shift)) & (t_id >= s_id)
    own_scores[...] = jnp.where(in_bucket, products, 0.0).astype(BF16)
    q_twice[:, :states] = q_ref[...]
    q_twice[:, states:] = q_ref[...]

    def near(c):
        here = v_ref[:, cols(c)].astype(F32)
        by_bucket = (here * spread(key_item[BUCKET], c)).astype(BF16)
        block = min(256, tokens)
        for start in range(0, tokens, block):
            rows = slice(start, start + block)
            acc[rows, cols(c)] = mm(own_scores[rows, rows], by_bucket[rows]) * spread(
                read_base, c, start, start + block
            )
        for level in range(1, near_levels + 1):
            run = BUCKET << (level - 1)
            for start in range(0, tokens, 2 * run):
                low = slice(start, start + run)
                high = slice(start + run, start + 2 * run)
                if run == BUCKET:
                    source = by_bucket[low]
                else:
                    source = (
                        here[low] * spread(key_item[run], c, start, start + run)
                    ).astype(BF16)
                acc[high, cols(c)] += mm(scores[high, low], source) * spread(
                    read_base + level, c, start + run, start + 2 * run
                )

    def far(level, payload, gap, c):
        state = payload[...] * jnp.exp(gap)
        high = state.astype(BF16)
        low = (state - high.astype(F32)).astype(BF16)
        acc[:, cols(c)] += mm(q_twice[...], jnp.concatenate([high, low], axis=0)) * spread(
            read_base + level, c
        )

    trailing = [
        (seq & ((1 << (t + 1)) - 1)) == (1 << t) - 1 for t in range(seq_bits)
    ]

    def tok_step(bit, c):
        tok_copy(bit, c).wait_recv()
        upper = ((tok >> bit) & 1) == 1
        mine, theirs = agg.at[bit, c], from_tok.at[bit, c]
        my_total, their_total = row_of(agg_total.at[bit], c), row_of(tok_total.at[bit], c)

        @pl.when(upper)
        def _():
            agg[bit + 1, c] = jnp.exp(my_total) * theirs[...] + mine[...]

        @pl.when(jnp.logical_not(upper))
        def _():
            agg[bit + 1, c] = jnp.exp(their_total) * mine[...] + theirs[...]

        if bit + 1 < tok_bits:
            tok_copy(bit + 1, c).start()

    def tok_totals(bit):
        tok_copy(bit, chunks).wait_recv()
        upper = ((tok >> bit) & 1) == 1
        agg_total[bit + 1] = agg_total[bit] + tok_total[bit]
        pref[bit + 1] = pref[bit] + jnp.where(upper, tok_total[bit], 0.0)
        if bit + 1 < tok_bits:
            tok_copy(bit + 1, chunks).start()

    def tok_read(bit, c):
        @pl.when(((tok >> bit) & 1) == 1)
        def _():
            far(near_levels + 1 + bit, from_tok.at[bit, c], row_of(pref.at[bit], c), c)

    sends_own = jnp.logical_and(has_next, trailing[0]) if seq_bits else None
    pref[0] = jnp.zeros(pref.shape[1:], F32)
    for bit in range(max(tok_bits, 1)):
        for c in range(chunks):
            if bit == 0:
                near(c)
            if bit < tok_bits:
                if c == 0:
                    tok_totals(bit)
                tok_step(bit, c)
            if bit + 1 >= tok_bits and seq_bits:

                @pl.when(sends_own)
                def _():
                    if c == 0:
                        seq_copy(agg_total.at[tok_bits], 0, chunks).start()
                    seq_copy(agg.at[tok_bits, c], 0, c).start()

            if bit < tok_bits:
                tok_read(bit, c)

    def held(slot):
        return ((seq >> slot) & 1) == 1

    def forwards(slot):
        return jnp.logical_and(has_next, ((seq + 1) >> slot) == (seq >> slot))

    def chains(slot):
        return jnp.logical_and(has_next, trailing[slot])

    def seq_totals(slot):
        stage = tok_bits + slot

        @pl.when(held(slot))
        def _():
            seq_copy(agg_total.at[tok_bits], slot, chunks).wait_recv()
            pref[stage + 1] = pref[stage] + seq_total[slot]

            @pl.when(forwards(slot))
            def _():
                seq_copy(seq_total.at[slot], slot, chunks).start()

            if slot + 1 < seq_bits:

                @pl.when(chains(slot + 1))
                def _():
                    total = agg_total[tok_bits]
                    for lower in range(slot + 1):
                        total = total + seq_total[lower]
                    chain_total[...] = total
                    seq_copy(chain_total, slot + 1, chunks).start()

        @pl.when(jnp.logical_not(held(slot)))
        def _():
            pref[stage + 1] = pref[stage]

    def seq_step(slot, c):
        @pl.when(held(slot))
        def _():
            seq_copy(agg.at[tok_bits, c], slot, c).wait_recv()

            @pl.when(forwards(slot))
            def _():
                seq_copy(from_seq.at[slot, c], slot, c).start()

            if splits(slot):
                swap_copy(slot, c, mine_at).start()

            if slot + 1 < seq_bits:

                @pl.when(chains(slot + 1))
                def _():
                    rows = pl.ds(mine_at, half) if splits(slot + 1) else slice(None)
                    total = row_of(agg_total.at[tok_bits], c)
                    state = agg[tok_bits, c, rows]
                    for lower in range(slot + 1):
                        state = state + jnp.exp(total) * from_seq[lower, c, rows]
                        total = total + row_of(seq_total.at[lower], c)
                    chain[c, rows] = state
                    seq_copy(chain.at[c], slot + 1, c).start()

    def seq_read(slot, c):
        @pl.when(held(slot))
        def _():
            if splits(slot):
                swap_copy(slot, c, other_at).wait_recv()
            far(
                near_levels + 1 + tok_bits + slot,
                from_seq.at[slot, c],
                row_of(pref.at[tok_bits + slot], c),
                c,
            )

    group_row = lax.broadcasted_iota(jnp.int32, (chunk, chunk), 0) >> head_shift
    group_col = lax.broadcasted_iota(jnp.int32, (chunk, chunk), 1) >> head_shift
    same_head = jnp.where(group_row == group_col, 1.0, 0.0).astype(BF16)

    def norm(c):
        y = acc[:, cols(c)]
        mean = mm((y * y).astype(BF16), same_head) * (1.0 / head_size)
        o_ref[:, cols(c)] = y * lax.rsqrt(mean + 1e-5)

    for slot in range(seq_bits):
        behind = 1 if splits(slot) else 0
        seq_totals(slot)
        for c in range(chunks + behind):
            if c < chunks:
                seq_step(slot, c)
            if c >= behind:
                seq_read(slot, c - behind)
                if slot == seq_bits - 1:
                    norm(c - behind)
    if not seq_bits:
        for c in range(chunks):
            norm(c)

    for bit in range(tok_bits):
        for c in range(chunks + 1):
            tok_copy(bit, c).wait_send()
    for slot in range(seq_bits):

        @pl.when(jnp.logical_and(has_next, (((seq + 1) >> slot) & 1) == 1))
        def _():
            for c in range(chunks + 1):
                source = seq_total.at[slot] if c == chunks else from_seq.at[slot, c]
                seq_copy(source, slot, c).wait_send()

        if splits(slot):

            @pl.when(held(slot))
            def _():
                for c in range(chunks):
                    swap_copy(slot, c, mine_at).wait_send()


def local(values, key_rows, query_rows, decay_codes, weight_codes, norm_gain):
    heads, tokens = decay_codes.shape
    columns = values.shape[1]
    states = key_rows.shape[1]
    head_size = columns // heads
    chunk = min(256, columns)
    chunks = columns // chunk
    tok_bits = lax.axis_size("tok").bit_length() - 1
    seq_bits = lax.axis_size("seq").bit_length() - 1
    near_levels = (tokens // BUCKET).bit_length() - 1
    per_group = 128 // (2 * heads)
    groups = -(-(near_levels + 1) // per_group) - (
        -(near_levels + 1 + tok_bits + seq_bits) // per_group
    )
    parcel = (chunks, states, chunk)
    totals = (columns // LANES, LANES)
    tok_slots, seq_slots = max(tok_bits, 1), max(seq_bits, 1)
    vmem = pl.BlockSpec(memory_space=pltpu.VMEM)
    normed = pl.pallas_call(
        functools.partial(kernel, (tok_bits, seq_bits, head_size, chunk)),
        out_shape=jax.ShapeDtypeStruct((tokens, columns), F32),
        in_specs=[pl.BlockSpec(memory_space=pltpu.HBM)] * 5,
        out_specs=vmem,
        scratch_shapes=[
            *(
                pltpu.VMEM(x.shape, x.dtype)
                for x in (values, key_rows, query_rows, decay_codes, weight_codes)
            ),
            pltpu.SemaphoreType.DMA((5,)),
            pltpu.VMEM((tokens, columns), F32),
            pltpu.VMEM((groups, tokens, LANES), BF16),
            pltpu.VMEM((per_group, LANES, columns), BF16),
            pltpu.VMEM((tokens, tokens), BF16),
            pltpu.VMEM((tokens, tokens), BF16),
            pltpu.VMEM((tokens, 2 * states), BF16),
            pltpu.VMEM((tok_bits + 1,) + parcel, F32),
            pltpu.VMEM((tok_slots,) + parcel, F32),
            pltpu.VMEM((seq_slots,) + parcel, F32),
            pltpu.VMEM(parcel, F32),
            pltpu.VMEM((tok_bits + seq_bits + 1,) + totals, F32),
            pltpu.VMEM((tok_bits + 1,) + totals, F32),
            pltpu.VMEM((tok_slots,) + totals, F32),
            pltpu.VMEM((seq_slots,) + totals, F32),
            pltpu.VMEM(totals, F32),
            pltpu.SemaphoreType.DMA((tok_slots, chunks + 1)),
            pltpu.SemaphoreType.DMA((tok_slots, chunks + 1)),
            pltpu.SemaphoreType.DMA((seq_slots, chunks + 1)),
            pltpu.SemaphoreType.DMA((seq_slots, chunks + 1)),
            pltpu.SemaphoreType.DMA((seq_slots, chunks)),
            pltpu.SemaphoreType.DMA((seq_slots, chunks)),
        ],
        compiler_params=pltpu.CompilerParams(
            collective_id=0, has_side_effects=True, vmem_limit_bytes=40 * 2**20
        ),
    )(values, key_rows, query_rows, decay_codes, weight_codes)
    return (normed * norm_gain[None, :]).astype(values.dtype)


def solution(mesh):
    return jax.shard_map(
        local,
        mesh=mesh,
        in_specs=(
            P(("parts", "seq", "tok"), "head"),
            P(("parts", "seq", "tok"), None),
            P(("parts", "seq", "tok"), None),
            P("head", ("parts", "seq", "tok")),
            P(None, "head", ("parts", "seq", "tok")),
            P("head"),
        ),
        out_specs=P(("parts", "seq", "tok"), "head"),
        check_vma=False,
    )
```

```python
import functools

import jax
import jax.numpy as jnp
from jax import lax
from jax.experimental import pallas as pl
from jax.experimental.pallas import tpu as pltpu
from jax.sharding import PartitionSpec as P

BUCKET = 64
F32 = jnp.float32
BF16 = jnp.bfloat16
MESH = pl.DeviceIdType.MESH
LANES = 128


def mm(a, b):
    return jnp.dot(a, b, preferred_element_type=F32)


def tmm(a, b):
    return lax.dot_general(a, b, (((0,), (0,)), ((), ())), preferred_element_type=F32)


def kernel(
    dims, v_hbm, k_hbm, q_hbm, codes_hbm, w_hbm, o_ref,
    v_ref, k_ref, q_ref, codes_ref, w_ref, load_sem,
    acc, items, sel, scores, own_scores, q_twice, agg, from_tok, from_seq, chain,
    pref, agg_total, tok_total, seq_total, chain_total,
    tok_send, tok_recv, seq_send, seq_recv, swap_send, swap_recv,
):
    tok_bits, seq_bits, head_size, chunk = dims
    heads, tokens = codes_ref.shape
    columns = v_ref.shape[1]
    states = k_ref.shape[1]
    chunks = columns // chunk
    near_levels = (tokens // BUCKET).bit_length() - 1
    per_group = 128 // (2 * heads)
    tok = lax.axis_index("tok")
    seq = lax.axis_index("seq")
    seq_count = 2**seq_bits
    has_next = seq + 1 < seq_count
    has_prev = seq > 0

    def load(i):
        source, target = (
            (codes_hbm, codes_ref), (k_hbm, k_ref), (v_hbm, v_ref), (q_hbm, q_ref), (w_hbm, w_ref)
        )[i]
        return pltpu.make_async_copy(source, target, load_sem.at[i])

    for i in range(5):
        load(i).start()

    barrier = pltpu.get_barrier_semaphore()
    for bit in range(tok_bits):
        pl.semaphore_signal(
            barrier, inc=1, device_id={"tok": tok ^ (1 << bit)}, device_id_type=MESH
        )

    @pl.when(has_next)
    def _():
        pl.semaphore_signal(barrier, inc=1, device_id={"seq": seq + 1}, device_id_type=MESH)

    @pl.when(has_prev)
    def _():
        pl.semaphore_signal(barrier, inc=1, device_id={"seq": seq - 1}, device_id_type=MESH)

    half = states // 2
    mine_at = pl.multiple_of((tok & 1) * half, half)
    other_at = pl.multiple_of((1 - (tok & 1)) * half, half)
    after_me = lax.rem(seq + 1, seq_count)

    def rows_of(part):
        return pl.ds(mine_at if part == 0 else other_at, half)

    def tok_copy(bit, c, part=0):
        if c == chunks:
            source, target = agg_total.at[bit], tok_total.at[bit]
            slot = 2 * chunks
        else:
            rows = rows_of(1 - part if bit == 0 else part)
            source, target = agg.at[bit, c, rows], from_tok.at[bit, c, rows]
            slot = 2 * c + part
        return pltpu.make_async_remote_copy(
            src_ref=source,
            dst_ref=target,
            send_sem=tok_send.at[bit, slot],
            recv_sem=tok_recv.at[bit, slot],
            device_id={"tok": tok ^ (1 << bit)},
            device_id_type=MESH,
        )

    def seq_copy(source, slot, c, part=0):
        if c == chunks:
            target = seq_total.at[slot]
            place = 2 * chunks
        else:
            source = source.at[rows_of(part)]
            target = from_seq.at[slot, c, rows_of(part)]
            place = 2 * c + part
        return pltpu.make_async_remote_copy(
            src_ref=source,
            dst_ref=target,
            send_sem=seq_send.at[slot, place],
            recv_sem=seq_recv.at[slot, place],
            device_id={"seq": after_me},
            device_id_type=MESH,
        )

    def swap_copy(slot, c, at):
        place = from_seq.at[slot, c, pl.ds(at, half)]
        return pltpu.make_async_remote_copy(
            src_ref=place,
            dst_ref=place,
            send_sem=swap_send.at[slot, c],
            recv_sem=swap_recv.at[slot, c],
            device_id={"tok": tok ^ 1},
            device_id_type=MESH,
        )

    pieces = chunk // LANES

    def row_of(total, c):
        return jnp.concatenate(
            [total[c * pieces + i : c * pieces + i + 1, :] for i in range(pieces)], axis=1
        )

    def cols(c):
        return slice(c * chunk, (c + 1) * chunk)

    load(0).wait()
    lane = lax.broadcasted_iota(jnp.int32, (heads, tokens), 1)
    run_total = codes_ref[...]
    prefix = run_total
    before, after = {}, {}
    size = 1
    while True:
        if size >= BUCKET:
            before[size] = prefix.astype(F32) * (-1.0 / 65536.0)
            after[size] = (run_total - prefix).astype(F32) * (-1.0 / 65536.0)
        if size == tokens:
            break
        upper = (lane & size) != 0
        lower_total = pltpu.roll(run_total, size, 1)
        upper_total = pltpu.roll(run_total, tokens - size, 1)
        prefix = prefix + jnp.where(upper, lower_total, 0)
        run_total = run_total + jnp.where(upper, lower_total, upper_total)
        size *= 2
    block_total = run_total.astype(F32) * (-1.0 / 65536.0)

    head_shift = head_size.bit_length() - 1
    item_shift = (2 * heads).bit_length() - 1

    def put_sel(i):
        row = lax.broadcasted_iota(jnp.int32, (LANES, columns), 0)
        column_head = lax.broadcasted_iota(jnp.int32, (LANES, columns), 1) >> head_shift
        wanted = ((row >> item_shift) == i) & ((row & (heads - 1)) == column_head)
        sel[i] = jnp.where(wanted, 1.0, 0.0).astype(BF16)

    put_sel(0)
    total_row = jnp.sum(
        jnp.where(
            lax.broadcasted_iota(jnp.int32, (heads, columns), 0)
            == lax.broadcasted_iota(jnp.int32, (heads, columns), 1) >> head_shift,
            block_total[:, :1],
            0.0,
        ),
        axis=0,
        keepdims=True,
    )

    def put_items(group, entries):
        halves = []
        for entry in entries:
            high = entry.astype(BF16).astype(F32)
            halves += [high, entry - high]
        short = per_group - len(entries)
        if short:
            halves.append(jnp.zeros((2 * heads * short, tokens), F32))
        items[group] = jnp.transpose(jnp.concatenate(halves, axis=0)).astype(BF16)

    def spread(index, c, start=0, stop=None):
        group, i = index // per_group, index % per_group
        stop = tokens if stop is None else stop
        return mm(items[group, start:stop, :], sel[i, :, cols(c)])

    sizes = [tokens] + [BUCKET << i for i in range(near_levels)]
    key_entries = [jnp.exp(after[s]) for s in sizes]
    key_groups = -(-len(key_entries) // per_group)
    for g in range(key_groups):
        put_items(g, key_entries[g * per_group : (g + 1) * per_group])
    key_item = {s: i for i, s in enumerate(sizes)}

    for r in range(columns // LANES):
        agg_total[0, r : r + 1] = total_row[:, r * LANES : (r + 1) * LANES]
    load(1).wait()
    load(2).wait()
    pl.semaphore_wait(
        barrier, tok_bits + has_next.astype(jnp.int32) + has_prev.astype(jnp.int32)
    )
    for c in range(chunks):
        decayed = (v_ref[:, cols(c)].astype(F32) * spread(0, c)).astype(BF16)
        agg[0, c] = tmm(k_ref[...], decayed)
        if c == 0:
            tok_copy(0, chunks).start()
        tok_copy(0, c, 0).start()
    for c in range(chunks):
        tok_copy(0, c, 1).start()
    for i in range(1, per_group):
        put_sel(i)

    load(3).wait()
    load(4).wait()

    def lam(level):
        return w_ref[level].astype(F32) * (1.0 / 256.0)

    read_entries = [lam(0) * jnp.exp(-after[BUCKET])]
    for level in range(1, near_levels + 1):
        read_entries.append(lam(level) * jnp.exp(before[BUCKET << (level - 1)]))
    since_start = jnp.exp(before[tokens])
    for level in range(near_levels + 1, near_levels + 1 + tok_bits + seq_bits):
        read_entries.append(lam(level) * since_start)
    read_base = key_groups * per_group
    for g in range(-(-len(read_entries) // per_group)):
        put_items(key_groups + g, read_entries[g * per_group : (g + 1) * per_group])

    products = lax.dot_general(
        q_ref[...], k_ref[...], (((1,), (1,)), ((), ())), preferred_element_type=F32
    )
    scores[...] = products.astype(BF16)
    t_id = lax.broadcasted_iota(jnp.int32, (tokens, tokens), 0)
    s_id = lax.broadcasted_iota(jnp.int32, (tokens, tokens), 1)
    bucket_shift = BUCKET.bit_length() - 1
    in_bucket = ((t_id >> bucket_shift) == (s_id >> bucket_shift)) & (t_id >= s_id)
    own_scores[...] = jnp.where(in_bucket, products, 0.0).astype(BF16)
    q_twice[:, :states] = q_ref[...]
    q_twice[:, states:] = q_ref[...]

    def near(c):
        here = v_ref[:, cols(c)].astype(F32)
        by_bucket = (here * spread(key_item[BUCKET], c)).astype(BF16)
        block = min(256, tokens)
        for start in range(0, tokens, block):
            rows = slice(start, start + block)
            acc[rows, cols(c)] = mm(own_scores[rows, rows], by_bucket[rows]) * spread(
                read_base, c, start, start + block
            )
        for level in range(1, near_levels + 1):
            run = BUCKET << (level - 1)
            for start in range(0, tokens, 2 * run):
                low = slice(start, start + run)
                high = slice(start + run, start + 2 * run)
                if run == BUCKET:
                    source = by_bucket[low]
                else:
                    source = (
                        here[low] * spread(key_item[run], c, start, start + run)
                    ).astype(BF16)
                acc[high, cols(c)] += mm(scores[high, low], source) * spread(
                    read_base + level, c, start + run, start + 2 * run
                )

    def far(level, payload, gap, c):
        state = payload[...] * jnp.exp(gap)
        high = state.astype(BF16)
        low = (state - high.astype(F32)).astype(BF16)
        acc[:, cols(c)] += mm(q_twice[...], jnp.concatenate([high, low], axis=0)) * spread(
            read_base + level, c
        )

    trailing = [
        (seq & ((1 << (t + 1)) - 1)) == (1 << t) - 1 for t in range(seq_bits)
    ]

    sends_own = jnp.logical_and(has_next, trailing[0]) if seq_bits else None

    def tok_step(bit, c, part):
        tok_copy(bit, c, part).wait_recv()
        upper = ((tok >> bit) & 1) == 1
        rows = rows_of(part)
        my_total, their_total = row_of(agg_total.at[bit], c), row_of(tok_total.at[bit], c)

        @pl.when(upper)
        def _():
            agg[bit + 1, c, rows] = (
                jnp.exp(my_total) * from_tok[bit, c, rows] + agg[bit, c, rows]
            )

        @pl.when(jnp.logical_not(upper))
        def _():
            agg[bit + 1, c, rows] = (
                jnp.exp(their_total) * agg[bit, c, rows] + from_tok[bit, c, rows]
            )

        if bit + 1 < tok_bits:
            tok_copy(bit + 1, c, part).start()
        elif seq_bits:

            @pl.when(sends_own)
            def _():
                if c == 0 and part == 0:
                    seq_copy(agg_total.at[tok_bits], 0, chunks).start()
                seq_copy(agg.at[tok_bits, c], 0, c, part).start()

    def tok_totals(bit):
        tok_copy(bit, chunks).wait_recv()
        upper = ((tok >> bit) & 1) == 1
        agg_total[bit + 1] = agg_total[bit] + tok_total[bit]
        pref[bit + 1] = pref[bit] + jnp.where(upper, tok_total[bit], 0.0)
        if bit + 1 < tok_bits:
            tok_copy(bit + 1, chunks).start()

    def tok_read(bit, c):
        @pl.when(((tok >> bit) & 1) == 1)
        def _():
            far(near_levels + 1 + bit, from_tok.at[bit, c], row_of(pref.at[bit], c), c)

    def held(slot):
        return ((seq >> slot) & 1) == 1

    def forwards(slot):
        return jnp.logical_and(has_next, ((seq + 1) >> slot) == (seq >> slot))

    def chains(slot):
        return jnp.logical_and(has_next, trailing[slot])

    def seq_totals(slot):
        stage = tok_bits + slot

        @pl.when(held(slot))
        def _():
            seq_copy(agg_total.at[tok_bits], slot, chunks).wait_recv()
            pref[stage + 1] = pref[stage] + seq_total[slot]

            @pl.when(forwards(slot))
            def _():
                seq_copy(seq_total.at[slot], slot, chunks).start()

            if slot + 1 < seq_bits:

                @pl.when(chains(slot + 1))
                def _():
                    total = agg_total[tok_bits]
                    for lower in range(slot + 1):
                        total = total + seq_total[lower]
                    chain_total[...] = total
                    seq_copy(chain_total, slot + 1, chunks).start()

        @pl.when(jnp.logical_not(held(slot)))
        def _():
            pref[stage + 1] = pref[stage]

    def seq_step(slot, c):
        @pl.when(held(slot))
        def _():
            seq_copy(agg.at[tok_bits, c], slot, c).wait_recv()

            if slot:

                @pl.when(forwards(slot))
                def _():
                    seq_copy(from_seq.at[slot, c], slot, c).start()

                swap_copy(slot, c, mine_at).start()

            if slot + 1 < seq_bits:

                @pl.when(chains(slot + 1))
                def _():
                    rows = rows_of(0)
                    total = row_of(agg_total.at[tok_bits], c)
                    state = agg[tok_bits, c, rows]
                    for lower in range(slot + 1):
                        state = state + jnp.exp(total) * from_seq[lower, c, rows]
                        total = total + row_of(seq_total.at[lower], c)
                    chain[c, rows] = state
                    seq_copy(chain.at[c], slot + 1, c).start()

    def seq_read(slot, c):
        @pl.when(held(slot))
        def _():
            if slot:
                swap_copy(slot, c, other_at).wait_recv()
            else:
                seq_copy(agg.at[tok_bits, c], 0, c, 1).wait_recv()
            far(
                near_levels + 1 + tok_bits + slot,
                from_seq.at[slot, c],
                row_of(pref.at[tok_bits + slot], c),
                c,
            )

    group_row = lax.broadcasted_iota(jnp.int32, (chunk, chunk), 0) >> head_shift
    group_col = lax.broadcasted_iota(jnp.int32, (chunk, chunk), 1) >> head_shift
    same_head = jnp.where(group_row == group_col, 1.0, 0.0).astype(BF16)

    def norm(c):
        y = acc[:, cols(c)]
        mean = mm((y * y).astype(BF16), same_head) * (1.0 / head_size)
        o_ref[:, cols(c)] = y * lax.rsqrt(mean + 1e-5)

    pref[0] = jnp.zeros(pref.shape[1:], F32)
    lag = min(2, chunks - 1)
    last = tok_bits - 1
    for bit in range(tok_bits):
        for c in range(chunks):
            if bit == 0:
                near(c)
            if c == 0:
                tok_totals(bit)
            tok_step(bit, c, 0)
            if bit == last and seq_bits and c >= lag:
                if c == lag:
                    seq_totals(0)
                seq_step(0, c - lag)
    for bit in range(last):
        for c in range(chunks):
            tok_step(bit, c, 1)
            tok_read(bit, c)
    for c in range(chunks + 1):
        if c < chunks:
            if seq_bits and c + chunks - lag < chunks:
                seq_step(0, c + chunks - lag)
            tok_step(last, c, 1)
            for slot in range(1, seq_bits):
                if c == 0:
                    seq_totals(slot)
                seq_step(slot, c)
            tok_read(last, c)
            if seq_bits:
                seq_read(0, c)
        if c > 0:
            for slot in range(1, seq_bits):
                seq_read(slot, c - 1)
            norm(c - 1)

    for bit in range(tok_bits):
        tok_copy(bit, chunks).wait_send()
        for c in range(chunks):
            for part in range(2):
                tok_copy(bit, c, part).wait_send()
    for slot in range(seq_bits):

        @pl.when(jnp.logical_and(has_next, (((seq + 1) >> slot) & 1) == 1))
        def _():
            seq_copy(seq_total.at[slot], slot, chunks).wait_send()
            for c in range(chunks):
                for part in range(1 if slot else 2):
                    seq_copy(from_seq.at[slot, c], slot, c, part).wait_send()

        if slot:

            @pl.when(held(slot))
            def _():
                for c in range(chunks):
                    swap_copy(slot, c, mine_at).wait_send()


def local(values, key_rows, query_rows, decay_codes, weight_codes, norm_gain):
    heads, tokens = decay_codes.shape
    columns = values.shape[1]
    states = key_rows.shape[1]
    head_size = columns // heads
    chunk = min(256, columns)
    chunks = columns // chunk
    tok_bits = lax.axis_size("tok").bit_length() - 1
    seq_bits = lax.axis_size("seq").bit_length() - 1
    assert tok_bits > 0
    near_levels = (tokens // BUCKET).bit_length() - 1
    per_group = 128 // (2 * heads)
    groups = -(-(near_levels + 1) // per_group) - (
        -(near_levels + 1 + tok_bits + seq_bits) // per_group
    )
    parcel = (chunks, states, chunk)
    totals = (columns // LANES, LANES)
    tok_slots, seq_slots = max(tok_bits, 1), max(seq_bits, 1)
    vmem = pl.BlockSpec(memory_space=pltpu.VMEM)
    normed = pl.pallas_call(
        functools.partial(kernel, (tok_bits, seq_bits, head_size, chunk)),
        out_shape=jax.ShapeDtypeStruct((tokens, columns), F32),
        in_specs=[pl.BlockSpec(memory_space=pltpu.HBM)] * 5,
        out_specs=vmem,
        scratch_shapes=[
            *(
                pltpu.VMEM(x.shape, x.dtype)
                for x in (values, key_rows, query_rows, decay_codes, weight_codes)
            ),
            pltpu.SemaphoreType.DMA((5,)),
            pltpu.VMEM((tokens, columns), F32),
            pltpu.VMEM((groups, tokens, LANES), BF16),
            pltpu.VMEM((per_group, LANES, columns), BF16),
            pltpu.VMEM((tokens, tokens), BF16),
            pltpu.VMEM((tokens, tokens), BF16),
            pltpu.VMEM((tokens, 2 * states), BF16),
            pltpu.VMEM((tok_bits + 1,) + parcel, F32),
            pltpu.VMEM((tok_slots,) + parcel, F32),
            pltpu.VMEM((seq_slots,) + parcel, F32),
            pltpu.VMEM(parcel, F32),
            pltpu.VMEM((tok_bits + seq_bits + 1,) + totals, F32),
            pltpu.VMEM((tok_bits + 1,) + totals, F32),
            pltpu.VMEM((tok_slots,) + totals, F32),
            pltpu.VMEM((seq_slots,) + totals, F32),
            pltpu.VMEM(totals, F32),
            pltpu.SemaphoreType.DMA((tok_slots, 2 * chunks + 1)),
            pltpu.SemaphoreType.DMA((tok_slots, 2 * chunks + 1)),
            pltpu.SemaphoreType.DMA((seq_slots, 2 * chunks + 1)),
            pltpu.SemaphoreType.DMA((seq_slots, 2 * chunks + 1)),
            pltpu.SemaphoreType.DMA((seq_slots, chunks)),
            pltpu.SemaphoreType.DMA((seq_slots, chunks)),
        ],
        compiler_params=pltpu.CompilerParams(
            collective_id=0, has_side_effects=True, vmem_limit_bytes=60000000
        ),
    )(values, key_rows, query_rows, decay_codes, weight_codes)
    return (normed * norm_gain[None, :]).astype(values.dtype)


def solution(mesh):
    return jax.shard_map(
        local,
        mesh=mesh,
        in_specs=(
            P(("parts", "seq", "tok"), "head"),
            P(("parts", "seq", "tok"), None),
            P(("parts", "seq", "tok"), None),
            P("head", ("parts", "seq", "tok")),
            P(None, "head", ("parts", "seq", "tok")),
            P("head"),
        ),
        out_specs=P(("parts", "seq", "tok"), "head"),
        check_vma=False,
    )
```

```python
import functools

import jax
import jax.numpy as jnp
from jax import lax
from jax.experimental import pallas as pl
from jax.experimental.pallas import tpu as pltpu
from jax.sharding import PartitionSpec as P

BUCKET = 64
F32 = jnp.float32
BF16 = jnp.bfloat16
MESH = pl.DeviceIdType.MESH
LANES = 128


def mm(a, b):
    return jnp.dot(a, b, preferred_element_type=F32)


def tmm(a, b):
    return lax.dot_general(a, b, (((0,), (0,)), ((), ())), preferred_element_type=F32)


def kernel(
    dims, v_hbm, k_hbm, q_hbm, codes_hbm, w_hbm, o_ref,
    v_ref, k_ref, q_ref, codes_ref, w_ref, load_sem,
    acc, items, sel, scores, own_scores, q_twice, agg, from_tok, from_seq, chain,
    pref, agg_total, tok_total, seq_total, chain_total,
    tok_send, tok_recv, seq_send, seq_recv, swap_send, swap_recv,
):
    tok_bits, seq_bits, head_size, chunk = dims
    heads, tokens = codes_ref.shape
    columns = v_ref.shape[1]
    states = k_ref.shape[1]
    chunks = columns // chunk
    near_levels = (tokens // BUCKET).bit_length() - 1
    per_group = 128 // (2 * heads)
    tok = lax.axis_index("tok")
    seq = lax.axis_index("seq")
    seq_count = 2**seq_bits
    has_next = seq + 1 < seq_count
    has_prev = seq > 0

    def load(i):
        source, target = (
            (codes_hbm, codes_ref), (k_hbm, k_ref), (v_hbm, v_ref), (q_hbm, q_ref), (w_hbm, w_ref)
        )[i]
        return pltpu.make_async_copy(source, target, load_sem.at[i])

    for i in range(5):
        load(i).start()

    barrier = pltpu.get_barrier_semaphore()
    for bit in range(tok_bits):
        pl.semaphore_signal(
            barrier, inc=1, device_id={"tok": tok ^ (1 << bit)}, device_id_type=MESH
        )

    @pl.when(has_next)
    def _():
        pl.semaphore_signal(barrier, inc=1, device_id={"seq": seq + 1}, device_id_type=MESH)

    @pl.when(has_prev)
    def _():
        pl.semaphore_signal(barrier, inc=1, device_id={"seq": seq - 1}, device_id_type=MESH)

    half = states // 2
    mine_at = pl.multiple_of((tok & 1) * half, half)
    other_at = pl.multiple_of((1 - (tok & 1)) * half, half)
    after_me = lax.rem(seq + 1, seq_count)

    def rows_of(part):
        return pl.ds(mine_at if part == 0 else other_at, half)

    def swaps(slot, c):
        return slot > 0 or c == 0

    def tok_copy(bit, c, part=0):
        if c == chunks:
            source, target = agg_total.at[bit], tok_total.at[bit]
            slot = 2 * chunks
        else:
            rows = rows_of(1 - part if bit == 0 else part)
            source, target = agg.at[bit, c, rows], from_tok.at[bit, c, rows]
            slot = 2 * c + part
        return pltpu.make_async_remote_copy(
            src_ref=source,
            dst_ref=target,
            send_sem=tok_send.at[bit, slot],
            recv_sem=tok_recv.at[bit, slot],
            device_id={"tok": tok ^ (1 << bit)},
            device_id_type=MESH,
        )

    def seq_copy(source, slot, c, part=0):
        if c == chunks:
            target = seq_total.at[slot]
            place = 2 * chunks
        else:
            source = source.at[rows_of(part)]
            target = from_seq.at[slot, c, rows_of(part)]
            place = 2 * c + part
        return pltpu.make_async_remote_copy(
            src_ref=source,
            dst_ref=target,
            send_sem=seq_send.at[slot, place],
            recv_sem=seq_recv.at[slot, place],
            device_id={"seq": after_me},
            device_id_type=MESH,
        )

    def swap_copy(slot, c, at):
        place = from_seq.at[slot, c, pl.ds(at, half)]
        return pltpu.make_async_remote_copy(
            src_ref=place,
            dst_ref=place,
            send_sem=swap_send.at[slot, c],
            recv_sem=swap_recv.at[slot, c],
            device_id={"tok": tok ^ 1},
            device_id_type=MESH,
        )

    pieces = chunk // LANES

    def row_of(total, c):
        return jnp.concatenate(
            [total[c * pieces + i : c * pieces + i + 1, :] for i in range(pieces)], axis=1
        )

    def cols(c):
        return slice(c * chunk, (c + 1) * chunk)

    head_shift = head_size.bit_length() - 1
    item_shift = (2 * heads).bit_length() - 1

    def put_sel(i):
        row = lax.broadcasted_iota(jnp.int32, (LANES, columns), 0)
        column_head = lax.broadcasted_iota(jnp.int32, (LANES, columns), 1) >> head_shift
        wanted = ((row >> item_shift) == i) & ((row & (heads - 1)) == column_head)
        sel[i] = jnp.where(wanted, 1.0, 0.0).astype(BF16)

    put_sel(0)
    load(0).wait()
    lane = lax.broadcasted_iota(jnp.int32, (heads, tokens), 1)
    run_total = codes_ref[...]
    prefix = run_total
    before, after = {}, {}
    size = 1
    while True:
        if size >= BUCKET:
            before[size] = prefix.astype(F32) * (-1.0 / 65536.0)
            after[size] = (run_total - prefix).astype(F32) * (-1.0 / 65536.0)
        if size == tokens:
            break
        upper = (lane & size) != 0
        lower_total = pltpu.roll(run_total, size, 1)
        upper_total = pltpu.roll(run_total, tokens - size, 1)
        prefix = prefix + jnp.where(upper, lower_total, 0)
        run_total = run_total + jnp.where(upper, lower_total, upper_total)
        size *= 2
    block_total = run_total.astype(F32) * (-1.0 / 65536.0)

    total_row = jnp.sum(
        jnp.where(
            lax.broadcasted_iota(jnp.int32, (heads, columns), 0)
            == lax.broadcasted_iota(jnp.int32, (heads, columns), 1) >> head_shift,
            block_total[:, :1],
            0.0,
        ),
        axis=0,
        keepdims=True,
    )

    def put_items(group, entries):
        halves = []
        for entry in entries:
            high = entry.astype(BF16).astype(F32)
            halves += [high, entry - high]
        short = per_group - len(entries)
        if short:
            halves.append(jnp.zeros((2 * heads * short, tokens), F32))
        items[group] = jnp.transpose(jnp.concatenate(halves, axis=0)).astype(BF16)

    def spread(index, c, start=0, stop=None):
        group, i = index // per_group, index % per_group
        stop = tokens if stop is None else stop
        return mm(items[group, start:stop, :], sel[i, :, cols(c)])

    sizes = [tokens] + [BUCKET << i for i in range(near_levels)]
    key_entries = [jnp.exp(after[s]) for s in sizes]
    key_groups = -(-len(key_entries) // per_group)
    for g in range(key_groups):
        put_items(g, key_entries[g * per_group : (g + 1) * per_group])
    key_item = {s: i for i, s in enumerate(sizes)}

    for r in range(columns // LANES):
        agg_total[0, r : r + 1] = total_row[:, r * LANES : (r + 1) * LANES]
    load(1).wait()
    load(2).wait()
    pl.semaphore_wait(
        barrier, tok_bits + has_next.astype(jnp.int32) + has_prev.astype(jnp.int32)
    )
    for c in range(chunks):
        decayed = (v_ref[:, cols(c)].astype(F32) * spread(0, c)).astype(BF16)
        agg[0, c] = tmm(k_ref[...], decayed)
        if c == 0:
            tok_copy(0, chunks).start()
        tok_copy(0, c, 0).start()
    for c in range(chunks):
        tok_copy(0, c, 1).start()
    for i in range(1, per_group):
        put_sel(i)

    load(3).wait()
    load(4).wait()

    def lam(level):
        return w_ref[level].astype(F32) * (1.0 / 256.0)

    read_entries = [lam(0) * jnp.exp(-after[BUCKET])]
    for level in range(1, near_levels + 1):
        read_entries.append(lam(level) * jnp.exp(before[BUCKET << (level - 1)]))
    since_start = jnp.exp(before[tokens])
    for level in range(near_levels + 1, near_levels + 1 + tok_bits + seq_bits):
        read_entries.append(lam(level) * since_start)
    read_base = key_groups * per_group
    for g in range(-(-len(read_entries) // per_group)):
        put_items(key_groups + g, read_entries[g * per_group : (g + 1) * per_group])

    products = lax.dot_general(
        q_ref[...], k_ref[...], (((1,), (1,)), ((), ())), preferred_element_type=F32
    )
    scores[...] = products.astype(BF16)
    t_id = lax.broadcasted_iota(jnp.int32, (tokens, tokens), 0)
    s_id = lax.broadcasted_iota(jnp.int32, (tokens, tokens), 1)
    bucket_shift = BUCKET.bit_length() - 1
    in_bucket = ((t_id >> bucket_shift) == (s_id >> bucket_shift)) & (t_id >= s_id)
    own_scores[...] = jnp.where(in_bucket, products, 0.0).astype(BF16)
    q_twice[:, :states] = q_ref[...]
    q_twice[:, states:] = q_ref[...]

    def near(c):
        here = v_ref[:, cols(c)].astype(F32)
        by_bucket = (here * spread(key_item[BUCKET], c)).astype(BF16)
        block = min(256, tokens)
        for start in range(0, tokens, block):
            rows = slice(start, start + block)
            acc[rows, cols(c)] = mm(own_scores[rows, rows], by_bucket[rows]) * spread(
                read_base, c, start, start + block
            )
        for level in range(1, near_levels + 1):
            run = BUCKET << (level - 1)
            for start in range(0, tokens, 2 * run):
                low = slice(start, start + run)
                high = slice(start + run, start + 2 * run)
                if run == BUCKET:
                    source = by_bucket[low]
                else:
                    source = (
                        here[low] * spread(key_item[run], c, start, start + run)
                    ).astype(BF16)
                acc[high, cols(c)] += mm(scores[high, low], source) * spread(
                    read_base + level, c, start + run, start + 2 * run
                )

    def far(level, payload, gap, c):
        state = payload[...] * jnp.exp(gap)
        high = state.astype(BF16)
        low = (state - high.astype(F32)).astype(BF16)
        acc[:, cols(c)] += mm(q_twice[...], jnp.concatenate([high, low], axis=0)) * spread(
            read_base + level, c
        )

    trailing = [
        (seq & ((1 << (t + 1)) - 1)) == (1 << t) - 1 for t in range(seq_bits)
    ]

    sends_own = jnp.logical_and(has_next, trailing[0]) if seq_bits else None

    def tok_step(bit, c, part):
        tok_copy(bit, c, part).wait_recv()
        upper = ((tok >> bit) & 1) == 1
        rows = rows_of(part)
        my_total, their_total = row_of(agg_total.at[bit], c), row_of(tok_total.at[bit], c)

        @pl.when(upper)
        def _():
            agg[bit + 1, c, rows] = (
                jnp.exp(my_total) * from_tok[bit, c, rows] + agg[bit, c, rows]
            )

        @pl.when(jnp.logical_not(upper))
        def _():
            agg[bit + 1, c, rows] = (
                jnp.exp(their_total) * agg[bit, c, rows] + from_tok[bit, c, rows]
            )

        if bit + 1 < tok_bits:
            tok_copy(bit + 1, c, part).start()
        elif seq_bits and part == 0:

            @pl.when(sends_own)
            def _():
                if c == 0:
                    seq_copy(agg_total.at[tok_bits], 0, chunks).start()
                seq_copy(agg.at[tok_bits, c], 0, c, 0).start()

    def tok_totals(bit):
        tok_copy(bit, chunks).wait_recv()
        upper = ((tok >> bit) & 1) == 1
        agg_total[bit + 1] = agg_total[bit] + tok_total[bit]
        pref[bit + 1] = pref[bit] + jnp.where(upper, tok_total[bit], 0.0)
        if bit + 1 < tok_bits:
            tok_copy(bit + 1, chunks).start()

    def tok_read(bit, c):
        @pl.when(((tok >> bit) & 1) == 1)
        def _():
            far(near_levels + 1 + bit, from_tok.at[bit, c], row_of(pref.at[bit], c), c)

    def held(slot):
        return ((seq >> slot) & 1) == 1

    def forwards(slot):
        return jnp.logical_and(has_next, ((seq + 1) >> slot) == (seq >> slot))

    def chains(slot):
        return jnp.logical_and(has_next, trailing[slot])

    def seq_totals(slot):
        stage = tok_bits + slot

        @pl.when(held(slot))
        def _():
            seq_copy(agg_total.at[tok_bits], slot, chunks).wait_recv()
            pref[stage + 1] = pref[stage] + seq_total[slot]

            @pl.when(forwards(slot))
            def _():
                seq_copy(seq_total.at[slot], slot, chunks).start()

            if slot + 1 < seq_bits:

                @pl.when(chains(slot + 1))
                def _():
                    total = agg_total[tok_bits]
                    for lower in range(slot + 1):
                        total = total + seq_total[lower]
                    chain_total[...] = total
                    seq_copy(chain_total, slot + 1, chunks).start()

        @pl.when(jnp.logical_not(held(slot)))
        def _():
            pref[stage + 1] = pref[stage]

    def seq_step(slot, c):
        @pl.when(held(slot))
        def _():
            seq_copy(agg.at[tok_bits, c], slot, c).wait_recv()

            if slot:

                @pl.when(forwards(slot))
                def _():
                    seq_copy(from_seq.at[slot, c], slot, c).start()

            if swaps(slot, c):
                swap_copy(slot, c, mine_at).start()

            if slot + 1 < seq_bits:

                @pl.when(chains(slot + 1))
                def _():
                    rows = rows_of(0)
                    total = row_of(agg_total.at[tok_bits], c)
                    state = agg[tok_bits, c, rows]
                    for lower in range(slot + 1):
                        state = state + jnp.exp(total) * from_seq[lower, c, rows]
                        total = total + row_of(seq_total.at[lower], c)
                    chain[c, rows] = state
                    seq_copy(chain.at[c], slot + 1, c).start()

    def seq_read(slot, c):
        @pl.when(held(slot))
        def _():
            if swaps(slot, c):
                swap_copy(slot, c, other_at).wait_recv()
            else:
                seq_copy(agg.at[tok_bits, c], 0, c, 1).wait_recv()
            far(
                near_levels + 1 + tok_bits + slot,
                from_seq.at[slot, c],
                row_of(pref.at[tok_bits + slot], c),
                c,
            )

    group_row = lax.broadcasted_iota(jnp.int32, (chunk, chunk), 0) >> head_shift
    group_col = lax.broadcasted_iota(jnp.int32, (chunk, chunk), 1) >> head_shift
    same_head = jnp.where(group_row == group_col, 1.0, 0.0).astype(BF16)

    def norm(c):
        y = acc[:, cols(c)]
        mean = mm((y * y).astype(BF16), same_head) * (1.0 / head_size)
        o_ref[:, cols(c)] = y * lax.rsqrt(mean + 1e-5)

    pref[0] = jnp.zeros(pref.shape[1:], F32)
    lag = min(2, chunks - 1)
    last = tok_bits - 1
    for bit in range(tok_bits):
        for c in range(chunks):
            if bit == 0:
                near(c)
            if c == 0:
                tok_totals(bit)
            tok_step(bit, c, 0)
            if bit == last and seq_bits and c >= lag:
                if c == lag:
                    seq_totals(0)
                seq_step(0, c - lag)
    for bit in range(last):
        for c in range(chunks):
            tok_step(bit, c, 1)
            tok_read(bit, c)
    for c in range(chunks + 1):
        if c < chunks:
            if seq_bits and c + chunks - lag < chunks:
                seq_step(0, c + chunks - lag)
            tok_step(last, c, 1)
            for slot in range(1, seq_bits):
                if c == 0:
                    seq_totals(slot)
                seq_step(slot, c)
            if seq_bits and not swaps(0, c):

                @pl.when(sends_own)
                def _():
                    seq_copy(agg.at[tok_bits, c], 0, c, 1).start()

            tok_read(last, c)
            if seq_bits:
                seq_read(0, c)
        if c > 0:
            for slot in range(1, seq_bits):
                seq_read(slot, c - 1)
            norm(c - 1)

    for bit in range(tok_bits):
        tok_copy(bit, chunks).wait_send()
        for c in range(chunks):
            for part in range(2):
                tok_copy(bit, c, part).wait_send()
    for slot in range(seq_bits):

        @pl.when(jnp.logical_and(has_next, (((seq + 1) >> slot) & 1) == 1))
        def _():
            seq_copy(seq_total.at[slot], slot, chunks).wait_send()
            for c in range(chunks):
                for part in range(1 if swaps(slot, c) else 2):
                    seq_copy(from_seq.at[slot, c], slot, c, part).wait_send()

        @pl.when(held(slot))
        def _():
            for c in range(chunks):
                if swaps(slot, c):
                    swap_copy(slot, c, mine_at).wait_send()


def local(values, key_rows, query_rows, decay_codes, weight_codes, norm_gain):
    heads, tokens = decay_codes.shape
    columns = values.shape[1]
    states = key_rows.shape[1]
    head_size = columns // heads
    chunk = min(256, columns)
    chunks = columns // chunk
    tok_bits = lax.axis_size("tok").bit_length() - 1
    seq_bits = lax.axis_size("seq").bit_length() - 1
    assert tok_bits > 0
    near_levels = (tokens // BUCKET).bit_length() - 1
    per_group = 128 // (2 * heads)
    groups = -(-(near_levels + 1) // per_group) - (
        -(near_levels + 1 + tok_bits + seq_bits) // per_group
    )
    parcel = (chunks, states, chunk)
    arrays = (values, key_rows, query_rows, decay_codes, weight_codes)
    totals = (columns // LANES, LANES)
    tok_slots, seq_slots = max(tok_bits, 1), max(seq_bits, 1)
    vmem = pl.BlockSpec(memory_space=pltpu.VMEM)
    normed = pl.pallas_call(
        functools.partial(kernel, (tok_bits, seq_bits, head_size, chunk)),
        out_shape=jax.ShapeDtypeStruct((tokens, columns), F32),
        in_specs=[pl.BlockSpec(memory_space=pltpu.HBM)] * 5,
        out_specs=vmem,
        scratch_shapes=[
            *(
                pltpu.VMEM(x.shape, x.dtype)
                for x in arrays
            ),
            pltpu.SemaphoreType.DMA((5,)),
            pltpu.VMEM((tokens, columns), F32),
            pltpu.VMEM((groups, tokens, LANES), BF16),
            pltpu.VMEM((per_group, LANES, columns), BF16),
            pltpu.VMEM((tokens, tokens), BF16),
            pltpu.VMEM((tokens, tokens), BF16),
            pltpu.VMEM((tokens, 2 * states), BF16),
            pltpu.VMEM((tok_bits + 1,) + parcel, F32),
            pltpu.VMEM((tok_slots,) + parcel, F32),
            pltpu.VMEM((seq_slots,) + parcel, F32),
            pltpu.VMEM(parcel, F32),
            pltpu.VMEM((tok_bits + seq_bits + 1,) + totals, F32),
            pltpu.VMEM((tok_bits + 1,) + totals, F32),
            pltpu.VMEM((tok_slots,) + totals, F32),
            pltpu.VMEM((seq_slots,) + totals, F32),
            pltpu.VMEM(totals, F32),
            pltpu.SemaphoreType.DMA((tok_slots, 2 * chunks + 1)),
            pltpu.SemaphoreType.DMA((tok_slots, 2 * chunks + 1)),
            pltpu.SemaphoreType.DMA((seq_slots, 2 * chunks + 1)),
            pltpu.SemaphoreType.DMA((seq_slots, 2 * chunks + 1)),
            pltpu.SemaphoreType.DMA((seq_slots, chunks)),
            pltpu.SemaphoreType.DMA((seq_slots, chunks)),
        ],
        compiler_params=pltpu.CompilerParams(
            collective_id=0, has_side_effects=True, vmem_limit_bytes=40 * 2**20
        ),
    )(*(pltpu.with_memory_space_constraint(x, pltpu.HBM) for x in arrays))
    return (normed * norm_gain[None, :]).astype(values.dtype)


def solution(mesh):
    return jax.shard_map(
        local,
        mesh=mesh,
        in_specs=(
            P(("parts", "seq", "tok"), "head"),
            P(("parts", "seq", "tok"), None),
            P(("parts", "seq", "tok"), None),
            P("head", ("parts", "seq", "tok")),
            P(None, "head", ("parts", "seq", "tok")),
            P("head"),
        ),
        out_specs=P(("parts", "seq", "tok"), "head"),
        check_vma=False,
    )
```

```python
import functools

import jax
import jax.numpy as jnp
from jax import lax
from jax.experimental import pallas as pl
from jax.experimental.pallas import tpu as pltpu
from jax.sharding import PartitionSpec as P

BUCKET = 64
F32 = jnp.float32
BF16 = jnp.bfloat16
MESH = pl.DeviceIdType.MESH
LANES = 128


def mm(a, b):
    return jnp.dot(a, b, preferred_element_type=F32)


def tmm(a, b):
    return lax.dot_general(a, b, (((0,), (0,)), ((), ())), preferred_element_type=F32)


def kernel(
    dims, v_hbm, k_hbm, q_hbm, codes_hbm, w_hbm, o_ref,
    v_ref, k_ref, q_ref, codes_ref, w_ref, load_sem,
    acc, items, sel, scores, own_scores, q_twice, agg, from_tok, from_seq, chain,
    pref, agg_total, tok_total, seq_total, chain_total,
    tok_send, tok_recv, seq_send, seq_recv, swap_send, swap_recv,
):
    tok_bits, seq_bits, head_size, chunk = dims
    heads, tokens = codes_ref.shape
    columns = v_ref.shape[1]
    states = k_ref.shape[1]
    chunks = columns // chunk
    near_levels = (tokens // BUCKET).bit_length() - 1
    per_group = 128 // (2 * heads)
    tok = lax.axis_index("tok")
    seq = lax.axis_index("seq")
    seq_count = 2**seq_bits
    has_next = seq + 1 < seq_count
    has_prev = seq > 0

    def load(i):
        source, target = (
            (codes_hbm, codes_ref), (k_hbm, k_ref), (v_hbm, v_ref), (q_hbm, q_ref), (w_hbm, w_ref)
        )[i]
        return pltpu.make_async_copy(source, target, load_sem.at[i])

    for i in range(5):
        load(i).start()

    barrier = pltpu.get_barrier_semaphore()
    for bit in range(tok_bits):
        pl.semaphore_signal(
            barrier, inc=1, device_id={"tok": tok ^ (1 << bit)}, device_id_type=MESH
        )

    @pl.when(has_next)
    def _():
        pl.semaphore_signal(barrier, inc=1, device_id={"seq": seq + 1}, device_id_type=MESH)

    @pl.when(has_prev)
    def _():
        pl.semaphore_signal(barrier, inc=1, device_id={"seq": seq - 1}, device_id_type=MESH)

    half = states // 2
    mine_at = pl.multiple_of((tok & 1) * half, half)
    other_at = pl.multiple_of((1 - (tok & 1)) * half, half)
    after_me = lax.rem(seq + 1, seq_count)

    def rows_of(part):
        return pl.ds(mine_at if part == 0 else other_at, half)

    def swaps(slot, c):
        return slot > 0 or c in (0, 2)

    def tok_copy(bit, c, part=0):
        if c == chunks:
            source, target = agg_total.at[bit], tok_total.at[bit]
            slot = 2 * chunks
        else:
            rows = rows_of(1 - part if bit == 0 else part)
            source, target = agg.at[bit, c, rows], from_tok.at[bit, c, rows]
            slot = 2 * c + part
        return pltpu.make_async_remote_copy(
            src_ref=source,
            dst_ref=target,
            send_sem=tok_send.at[bit, slot],
            recv_sem=tok_recv.at[bit, slot],
            device_id={"tok": tok ^ (1 << bit)},
            device_id_type=MESH,
        )

    def seq_copy(source, slot, c, part=0):
        if c == chunks:
            target = seq_total.at[slot]
            place = 2 * chunks
        else:
            source = source.at[rows_of(part)]
            target = from_seq.at[slot, c, rows_of(part)]
            place = 2 * c + part
        return pltpu.make_async_remote_copy(
            src_ref=source,
            dst_ref=target,
            send_sem=seq_send.at[slot, place],
            recv_sem=seq_recv.at[slot, place],
            device_id={"seq": after_me},
            device_id_type=MESH,
        )

    def swap_copy(slot, c, at):
        place = from_seq.at[slot, c, pl.ds(at, half)]
        return pltpu.make_async_remote_copy(
            src_ref=place,
            dst_ref=place,
            send_sem=swap_send.at[slot, c],
            recv_sem=swap_recv.at[slot, c],
            device_id={"tok": tok ^ 1},
            device_id_type=MESH,
        )

    pieces = chunk // LANES

    def row_of(total, c):
        return jnp.concatenate(
            [total[c * pieces + i : c * pieces + i + 1, :] for i in range(pieces)], axis=1
        )

    def cols(c):
        return slice(c * chunk, (c + 1) * chunk)

    head_shift = head_size.bit_length() - 1
    item_shift = (2 * heads).bit_length() - 1

    def put_sel(i):
        row = lax.broadcasted_iota(jnp.int32, (LANES, columns), 0)
        column_head = lax.broadcasted_iota(jnp.int32, (LANES, columns), 1) >> head_shift
        wanted = ((row >> item_shift) == i) & ((row & (heads - 1)) == column_head)
        sel[i] = jnp.where(wanted, 1.0, 0.0).astype(BF16)

    put_sel(0)
    load(0).wait()
    lane = lax.broadcasted_iota(jnp.int32, (heads, tokens), 1)
    run_total = codes_ref[...]
    prefix = run_total
    before, after = {}, {}
    size = 1
    while True:
        if size >= BUCKET:
            before[size] = prefix.astype(F32) * (-1.0 / 65536.0)
            after[size] = (run_total - prefix).astype(F32) * (-1.0 / 65536.0)
        if size == tokens:
            break
        upper = (lane & size) != 0
        lower_total = pltpu.roll(run_total, size, 1)
        upper_total = pltpu.roll(run_total, tokens - size, 1)
        prefix = prefix + jnp.where(upper, lower_total, 0)
        run_total = run_total + jnp.where(upper, lower_total, upper_total)
        size *= 2
    block_total = run_total.astype(F32) * (-1.0 / 65536.0)

    total_row = jnp.sum(
        jnp.where(
            lax.broadcasted_iota(jnp.int32, (heads, columns), 0)
            == lax.broadcasted_iota(jnp.int32, (heads, columns), 1) >> head_shift,
            block_total[:, :1],
            0.0,
        ),
        axis=0,
        keepdims=True,
    )

    def put_items(group, entries):
        halves = []
        for entry in entries:
            high = entry.astype(BF16).astype(F32)
            halves += [high, entry - high]
        short = per_group - len(entries)
        if short:
            halves.append(jnp.zeros((2 * heads * short, tokens), F32))
        items[group] = jnp.transpose(jnp.concatenate(halves, axis=0)).astype(BF16)

    def spread(index, c, start=0, stop=None):
        group, i = index // per_group, index % per_group
        stop = tokens if stop is None else stop
        return mm(items[group, start:stop, :], sel[i, :, cols(c)])

    sizes = [tokens] + [BUCKET << i for i in range(near_levels)]
    key_entries = [jnp.exp(after[s]) for s in sizes]
    key_groups = -(-len(key_entries) // per_group)
    for g in range(key_groups):
        put_items(g, key_entries[g * per_group : (g + 1) * per_group])
    key_item = {s: i for i, s in enumerate(sizes)}

    for r in range(columns // LANES):
        agg_total[0, r : r + 1] = total_row[:, r * LANES : (r + 1) * LANES]
    load(1).wait()
    load(2).wait()
    pl.semaphore_wait(
        barrier, tok_bits + has_next.astype(jnp.int32) + has_prev.astype(jnp.int32)
    )
    for c in range(chunks):
        decayed = (v_ref[:, cols(c)].astype(F32) * spread(0, c)).astype(BF16)
        agg[0, c] = tmm(k_ref[...], decayed)
        if c == 0:
            tok_copy(0, chunks).start()
        tok_copy(0, c, 0).start()
    for c in range(chunks):
        tok_copy(0, c, 1).start()
    for i in range(1, per_group):
        put_sel(i)

    load(3).wait()
    load(4).wait()

    def lam(level):
        return w_ref[level].astype(F32) * (1.0 / 256.0)

    read_entries = [lam(0) * jnp.exp(-after[BUCKET])]
    for level in range(1, near_levels + 1):
        read_entries.append(lam(level) * jnp.exp(before[BUCKET << (level - 1)]))
    since_start = jnp.exp(before[tokens])
    for level in range(near_levels + 1, near_levels + 1 + tok_bits + seq_bits):
        read_entries.append(lam(level) * since_start)
    read_base = key_groups * per_group
    for g in range(-(-len(read_entries) // per_group)):
        put_items(key_groups + g, read_entries[g * per_group : (g + 1) * per_group])

    products = lax.dot_general(
        q_ref[...], k_ref[...], (((1,), (1,)), ((), ())), preferred_element_type=F32
    )
    scores[...] = products.astype(BF16)
    t_id = lax.broadcasted_iota(jnp.int32, (tokens, tokens), 0)
    s_id = lax.broadcasted_iota(jnp.int32, (tokens, tokens), 1)
    bucket_shift = BUCKET.bit_length() - 1
    in_bucket = ((t_id >> bucket_shift) == (s_id >> bucket_shift)) & (t_id >= s_id)
    own_scores[...] = jnp.where(in_bucket, products, 0.0).astype(BF16)
    q_twice[:, :states] = q_ref[...]
    q_twice[:, states:] = q_ref[...]

    def near(c):
        here = v_ref[:, cols(c)].astype(F32)
        by_bucket = (here * spread(key_item[BUCKET], c)).astype(BF16)
        block = min(256, tokens)
        for start in range(0, tokens, block):
            rows = slice(start, start + block)
            acc[rows, cols(c)] = mm(own_scores[rows, rows], by_bucket[rows]) * spread(
                read_base, c, start, start + block
            )
        for level in range(1, near_levels + 1):
            run = BUCKET << (level - 1)
            for start in range(0, tokens, 2 * run):
                low = slice(start, start + run)
                high = slice(start + run, start + 2 * run)
                if run == BUCKET:
                    source = by_bucket[low]
                else:
                    source = (
                        here[low] * spread(key_item[run], c, start, start + run)
                    ).astype(BF16)
                acc[high, cols(c)] += mm(scores[high, low], source) * spread(
                    read_base + level, c, start + run, start + 2 * run
                )

    def far(level, payload, gap, c):
        state = payload[...] * jnp.exp(gap)
        high = state.astype(BF16)
        low = (state - high.astype(F32)).astype(BF16)
        acc[:, cols(c)] += mm(q_twice[...], jnp.concatenate([high, low], axis=0)) * spread(
            read_base + level, c
        )

    trailing = [
        (seq & ((1 << (t + 1)) - 1)) == (1 << t) - 1 for t in range(seq_bits)
    ]

    sends_own = jnp.logical_and(has_next, trailing[0]) if seq_bits else None

    def tok_step(bit, c, part):
        tok_copy(bit, c, part).wait_recv()
        upper = ((tok >> bit) & 1) == 1
        rows = rows_of(part)
        my_total, their_total = row_of(agg_total.at[bit], c), row_of(tok_total.at[bit], c)

        @pl.when(upper)
        def _():
            agg[bit + 1, c, rows] = (
                jnp.exp(my_total) * from_tok[bit, c, rows] + agg[bit, c, rows]
            )

        @pl.when(jnp.logical_not(upper))
        def _():
            agg[bit + 1, c, rows] = (
                jnp.exp(their_total) * agg[bit, c, rows] + from_tok[bit, c, rows]
            )

        if bit + 1 < tok_bits:
            tok_copy(bit + 1, c, part).start()
        elif seq_bits and part == 0:

            @pl.when(sends_own)
            def _():
                if c == 0:
                    seq_copy(agg_total.at[tok_bits], 0, chunks).start()
                seq_copy(agg.at[tok_bits, c], 0, c, 0).start()

    def tok_totals(bit):
        tok_copy(bit, chunks).wait_recv()
        upper = ((tok >> bit) & 1) == 1
        agg_total[bit + 1] = agg_total[bit] + tok_total[bit]
        pref[bit + 1] = pref[bit] + jnp.where(upper, tok_total[bit], 0.0)
        if bit + 1 < tok_bits:
            tok_copy(bit + 1, chunks).start()

    def tok_read(bit, c):
        @pl.when(((tok >> bit) & 1) == 1)
        def _():
            far(near_levels + 1 + bit, from_tok.at[bit, c], row_of(pref.at[bit], c), c)

    def held(slot):
        return ((seq >> slot) & 1) == 1

    def forwards(slot):
        return jnp.logical_and(has_next, ((seq + 1) >> slot) == (seq >> slot))

    def chains(slot):
        return jnp.logical_and(has_next, trailing[slot])

    def seq_totals(slot):
        stage = tok_bits + slot

        @pl.when(held(slot))
        def _():
            seq_copy(agg_total.at[tok_bits], slot, chunks).wait_recv()
            pref[stage + 1] = pref[stage] + seq_total[slot]

            @pl.when(forwards(slot))
            def _():
                seq_copy(seq_total.at[slot], slot, chunks).start()

            if slot + 1 < seq_bits:

                @pl.when(chains(slot + 1))
                def _():
                    total = agg_total[tok_bits]
                    for lower in range(slot + 1):
                        total = total + seq_total[lower]
                    chain_total[...] = total
                    seq_copy(chain_total, slot + 1, chunks).start()

        @pl.when(jnp.logical_not(held(slot)))
        def _():
            pref[stage + 1] = pref[stage]

    def seq_step(slot, c):
        @pl.when(held(slot))
        def _():
            seq_copy(agg.at[tok_bits, c], slot, c).wait_recv()

            if slot:

                @pl.when(forwards(slot))
                def _():
                    seq_copy(from_seq.at[slot, c], slot, c).start()

            if swaps(slot, c):
                swap_copy(slot, c, mine_at).start()

            if slot + 1 < seq_bits:

                @pl.when(chains(slot + 1))
                def _():
                    rows = rows_of(0)
                    total = row_of(agg_total.at[tok_bits], c)
                    state = agg[tok_bits, c, rows]
                    for lower in range(slot + 1):
                        state = state + jnp.exp(total) * from_seq[lower, c, rows]
                        total = total + row_of(seq_total.at[lower], c)
                    chain[c, rows] = state
                    seq_copy(chain.at[c], slot + 1, c).start()

    def seq_read(slot, c):
        @pl.when(held(slot))
        def _():
            if swaps(slot, c):
                swap_copy(slot, c, other_at).wait_recv()
            else:
                seq_copy(agg.at[tok_bits, c], 0, c, 1).wait_recv()
            far(
                near_levels + 1 + tok_bits + slot,
                from_seq.at[slot, c],
                row_of(pref.at[tok_bits + slot], c),
                c,
            )

    group_row = lax.broadcasted_iota(jnp.int32, (chunk, chunk), 0) >> head_shift
    group_col = lax.broadcasted_iota(jnp.int32, (chunk, chunk), 1) >> head_shift
    same_head = jnp.where(group_row == group_col, 1.0, 0.0).astype(BF16)

    def norm(c):
        y = acc[:, cols(c)]
        mean = mm((y * y).astype(BF16), same_head) * (1.0 / head_size)
        o_ref[:, cols(c)] = y * lax.rsqrt(mean + 1e-5)

    pref[0] = jnp.zeros(pref.shape[1:], F32)
    lag = min(1, chunks - 1)
    last = tok_bits - 1
    for bit in range(tok_bits):
        for c in range(chunks):
            if bit == 0:
                near(c)
            if c == 0:
                tok_totals(bit)
            tok_step(bit, c, 0)
            if bit == last and seq_bits and c >= lag:
                if c == lag:
                    seq_totals(0)
                seq_step(0, c - lag)
    for bit in range(last):
        for c in range(chunks):
            tok_step(bit, c, 1)
            tok_read(bit, c)
    for c in range(chunks + 1):
        if c < chunks:
            if seq_bits and c + chunks - lag < chunks:
                seq_step(0, c + chunks - lag)
            tok_step(last, c, 1)
            for slot in range(1, seq_bits):
                if c == 0:
                    seq_totals(slot)
                seq_step(slot, c)
            if seq_bits and not swaps(0, c):

                @pl.when(sends_own)
                def _():
                    seq_copy(agg.at[tok_bits, c], 0, c, 1).start()

            tok_read(last, c)
            if seq_bits:
                seq_read(0, c)
        if c > 0:
            for slot in range(1, seq_bits):
                seq_read(slot, c - 1)
            norm(c - 1)

    for bit in range(tok_bits):
        tok_copy(bit, chunks).wait_send()
        for c in range(chunks):
            for part in range(2):
                tok_copy(bit, c, part).wait_send()
    for slot in range(seq_bits):

        @pl.when(jnp.logical_and(has_next, (((seq + 1) >> slot) & 1) == 1))
        def _():
            seq_copy(seq_total.at[slot], slot, chunks).wait_send()
            for c in range(chunks):
                for part in range(1 if swaps(slot, c) else 2):
                    seq_copy(from_seq.at[slot, c], slot, c, part).wait_send()

        @pl.when(held(slot))
        def _():
            for c in range(chunks):
                if swaps(slot, c):
                    swap_copy(slot, c, mine_at).wait_send()


def local(values, key_rows, query_rows, decay_codes, weight_codes, norm_gain):
    heads, tokens = decay_codes.shape
    columns = values.shape[1]
    states = key_rows.shape[1]
    head_size = columns // heads
    chunk = min(256, columns)
    chunks = columns // chunk
    tok_bits = lax.axis_size("tok").bit_length() - 1
    seq_bits = lax.axis_size("seq").bit_length() - 1
    assert tok_bits > 0
    near_levels = (tokens // BUCKET).bit_length() - 1
    per_group = 128 // (2 * heads)
    groups = -(-(near_levels + 1) // per_group) - (
        -(near_levels + 1 + tok_bits + seq_bits) // per_group
    )
    parcel = (chunks, states, chunk)
    arrays = (values, key_rows, query_rows, decay_codes, weight_codes)
    totals = (columns // LANES, LANES)
    tok_slots, seq_slots = max(tok_bits, 1), max(seq_bits, 1)
    vmem = pl.BlockSpec(memory_space=pltpu.VMEM)
    normed = pl.pallas_call(
        functools.partial(kernel, (tok_bits, seq_bits, head_size, chunk)),
        out_shape=jax.ShapeDtypeStruct((tokens, columns), F32),
        in_specs=[pl.BlockSpec(memory_space=pltpu.HBM)] * 5,
        out_specs=vmem,
        scratch_shapes=[
            *(
                pltpu.VMEM(x.shape, x.dtype)
                for x in arrays
            ),
            pltpu.SemaphoreType.DMA((5,)),
            pltpu.VMEM((tokens, columns), F32),
            pltpu.VMEM((groups, tokens, LANES), BF16),
            pltpu.VMEM((per_group, LANES, columns), BF16),
            pltpu.VMEM((tokens, tokens), BF16),
            pltpu.VMEM((tokens, tokens), BF16),
            pltpu.VMEM((tokens, 2 * states), BF16),
            pltpu.VMEM((tok_bits + 1,) + parcel, F32),
            pltpu.VMEM((tok_slots,) + parcel, F32),
            pltpu.VMEM((seq_slots,) + parcel, F32),
            pltpu.VMEM(parcel, F32),
            pltpu.VMEM((tok_bits + seq_bits + 1,) + totals, F32),
            pltpu.VMEM((tok_bits + 1,) + totals, F32),
            pltpu.VMEM((tok_slots,) + totals, F32),
            pltpu.VMEM((seq_slots,) + totals, F32),
            pltpu.VMEM(totals, F32),
            pltpu.SemaphoreType.DMA((tok_slots, 2 * chunks + 1)),
            pltpu.SemaphoreType.DMA((tok_slots, 2 * chunks + 1)),
            pltpu.SemaphoreType.DMA((seq_slots, 2 * chunks + 1)),
            pltpu.SemaphoreType.DMA((seq_slots, 2 * chunks + 1)),
            pltpu.SemaphoreType.DMA((seq_slots, chunks)),
            pltpu.SemaphoreType.DMA((seq_slots, chunks)),
        ],
        compiler_params=pltpu.CompilerParams(
            collective_id=0, has_side_effects=True, vmem_limit_bytes=40 * 2**20
        ),
    )(*(pltpu.with_memory_space_constraint(x, pltpu.HBM) for x in arrays))
    return (normed * norm_gain[None, :]).astype(values.dtype)


def solution(mesh):
    return jax.shard_map(
        local,
        mesh=mesh,
        in_specs=(
            P(("parts", "seq", "tok"), "head"),
            P(("parts", "seq", "tok"), None),
            P(("parts", "seq", "tok"), None),
            P("head", ("parts", "seq", "tok")),
            P(None, "head", ("parts", "seq", "tok")),
            P("head"),
        ),
        out_specs=P(("parts", "seq", "tok"), "head"),
        check_vma=False,
    )
```
